32 devices in a mesh: az: 4 (over y, x), ax: 8 (over z, core).
Axes of the slice: x: 2, y: 2, z: 4, core: 2. Of those that a mesh axis runs over, the one named last changes fastest.
Arguments:
- section_state: float32 [4, 128, 512, 256], P(None, 'az', 'ax'), may hold values from -6 to 6
- base_state: float32 [4, 128, 512, 256], P(None, 'az', 'ax'), may hold values from -6 to 6
- axial_flow: float32 [128, 512, 256], P('az', 'ax'), may hold values from 0.2 to 0.8
- fin_state: float32 [2048, 4, 256], P(('az', 'ax')), may hold values from -6 to 6
- receptor_rows: int32 [4096], P(('az', 'ax')), may hold values from 0 to 2047, as said below
- donor_owner: int32 [4096, 1], P(('az', 'ax')), may hold values from 0 to 31; in each aligned block of 128 rows (0 to 127, 128 to 255, ...) at most 8 rows name the same one
- donor_local: int32 [4096], P(('az', 'ax')), may hold values from 0 to 62
- interp_weights: float32 [4096, 2], P(('az', 'ax')), may hold values from 0 to 1
Outputs:
- next_state: float32 [4, 128, 512, 256], P(None, 'az', 'ax')
The draws below stay inside these ranges and needn't reach their ends.
Inputs may be any that keep to these rules, and one draw needn't show every extreme that they name: `receptor_rows`: within each device's block of 128 entries the rows are distinct. `donor_owner`: within each device's block of 128 receptors no owner is named more than 8 times.
All inputs are finite; a program needn't handle non-finite values.
Results may differ from the reference program's by a relative error of at most 0.00002.
Values sent between devices are 32-bit elements; how exact they have to be, the bound alone decides.
No kernel may reach another device: no remote copies, remote signals or barrier semaphores. Data moves between devices by JAX's collectives and lax.ppermute only.
A program may use at most 320 MiB of HBM per device.

```python
import math
import jax
import jax.numpy as jnp
import numpy as np
from jax import lax

TH_DEV = 32
Z_DEV = 64
NR = 256
COMPONENTS = 4
FIN_DEV = 64
REC_DEV = 128
CAP = 8
NTH = 128
NZ = 512
FIN_ROWS = 2048
RECEPTORS = 4096
N_AZ = 4
N_AX = 8


def draw_receptor_rows(key, part):
    rows_dev = TH_DEV * Z_DEV
    blocks = RECEPTORS // REC_DEV
    keys = jax.random.split(key, blocks)

    def draw_block(subkey):
        first_key, second_key = jax.random.split(subkey)
        inside = jax.random.permutation(first_key, rows_dev - 2)[:REC_DEV - 2] + 1
        chosen = jnp.concatenate([jnp.array([0, rows_dev - 1], dtype=jnp.int32), inside.astype(jnp.int32)])
        return jax.random.permutation(second_key, chosen)
    return jax.vmap(draw_block)(keys).reshape(-1).astype(jnp.int32)


def set_ends(values, key, least, high):
    index_at = [jax.random.randint(jax.random.fold_in(key, axis), (), 0, length) for axis, length in enumerate(values.shape)]
    main_axis = values.shape.index(max(values.shape))
    neighbour = index_at[:main_axis] + [(index_at[main_axis] + 1) % values.shape[main_axis]] + index_at[main_axis + 1:]
    return values.at[tuple(index_at)].set(least).at[tuple(neighbour)].set(high)


def block_scale(rng, dims, cuts, least, largest):
    def one(position, shards_of):
        draws = jax.random.uniform(jax.random.fold_in(jax.random.fold_in(rng, 6), position), (shards_of,), jnp.float32, least / len(cuts), largest / len(cuts))
        return jnp.repeat(jnp.exp(draws), dims[position] // shards_of).reshape((-1,) + (1,) * (len(dims) - position - 1))

    level = one(*cuts[0])
    for cut in cuts[1:]:
        level = level * one(*cut)
    return level


def routed_block(own_key, own, number, rows, amount, top, most, skew):
    sequence = jax.random.permutation(own_key, amount)
    heavy_load, common = portions_of(amount, rows * top, most, skew, True), portions_of(amount, rows * top, most, skew, False)
    places = jnp.arange(amount)

    def named(tallies, rotation):
        used = int((tallies > 0).sum())
        fixed = max(1, used // 4)
        shifted = fixed + (places - fixed + rotation * (used - fixed)) % max(1, amount - fixed)
        return jnp.zeros((amount,), jnp.int32).at[sequence[jnp.where(places < fixed, places, shifted)]].set(jnp.asarray(tallies, jnp.int32))

    tallies = jnp.where(number % 4 == 0, named(heavy_load, number // 4), named(common, number - number // 4 - 1))
    mixed = jax.random.permutation(jax.random.fold_in(own, 3), amount)
    giver, taker = mixed[0:amount // 2 * 2:2], mixed[1:amount // 2 * 2:2]
    slack = jnp.minimum(tallies[giver] - 1, most - tallies[taker]) // 2
    slack = jnp.where((giver == sequence[0]) | (taker == sequence[0]) | (tallies[taker] == 0), 0, jnp.maximum(slack, 0))
    shifted = jax.random.randint(jax.random.fold_in(own, 4), (amount // 2,), 0, 1 << 20) % (slack + 1)
    tallies = tallies.at[giver].add(-shifted).at[taker].add(shifted)
    items = jnp.searchsorted(jnp.cumsum(tallies), jnp.arange(rows * top), side="right").astype(jnp.int32)
    table = items.reshape(top, rows).T
    table = table[jax.random.permutation(jax.random.fold_in(own, 1), rows)]
    rotation = jax.random.randint(jax.random.fold_in(own, 2), (rows, 1), 0, top)
    return jnp.take_along_axis(table, (jnp.arange(top)[None, :] + rotation) % top, axis=1)


def portions_of(amount, total, reach, skew, full):
    portions = [(1 << 20) // math.isqrt(grade ** skew) + 1 for grade in range(1, amount + 1)]
    largest = reach if full else min(reach, max(-(-total // amount), total * portions[0] // sum(portions)))
    least = 1 if total - largest >= amount - 1 else 0
    holding, spare = [largest] + [least] * (amount - 1), total - largest - least * (amount - 1)
    while spare > 0:
        free = [i for i in range(1, amount) if holding[i] < largest] or [i for i in range(1, amount) if holding[i] < reach]
        whole, left = sum([portions[i] for i in free]), spare
        for i in free:
            more = min(reach - holding[i], max(1, left * portions[i] // whole), spare)
            holding[i] = holding[i] + more
            spare = spare - more
    return np.array(holding)


def gaussian(own_key, extent, spread, reach, cuts=(), held_as=jnp.bfloat16):
    values = spread * jax.random.normal(own_key, extent, jnp.float32)
    if cuts:
        values = values * block_scale(own_key, extent, cuts, -0.22, 0.18)
    return jnp.clip(values, -reach, reach).astype(held_as)


def setup_inputs(seed: int = 0) -> dict:
    seeds = jax.random.split(jax.random.key(seed), 9)
    section_state = gaussian(seeds[0], (COMPONENTS, NTH, NZ, NR), 1.0, 6.0, ((1, 4), (2, 8)), jnp.float32)
    base_state = gaussian(seeds[1], (COMPONENTS, NTH, NZ, NR), 1.0, 6.0, ((1, 4), (2, 8)), jnp.float32)
    axial_flow = jnp.clip(0.2 + 0.6 * jax.random.uniform(seeds[2], (NTH, NZ, NR), jnp.float32) ** block_scale(seeds[2], (NTH, NZ, NR), ((0, 4), (1, 8)), -0.2, 0.2), 0.2, 0.8)
    fin_state = gaussian(seeds[3], (FIN_ROWS, COMPONENTS, NR), 1.0, 6.0, ((0, 32),), jnp.float32)
    receptor_rows = draw_receptor_rows(jax.random.fold_in(seeds[8], 71), 0)
    donor_owner_keys = jax.random.split(jax.random.fold_in(seeds[5], 1), RECEPTORS // REC_DEV)
    donor_owner_turns = jax.random.permutation(jax.random.fold_in(seeds[5], 3), RECEPTORS // REC_DEV)
    donor_owner = jax.vmap(lambda own, number: routed_block(jax.random.fold_in(seeds[5], 2), own, number, REC_DEV, N_AZ * N_AX, 1, CAP, 2))(donor_owner_keys, donor_owner_turns).reshape((RECEPTORS, 1))
    donor_local = set_ends(jax.random.randint(seeds[6], (RECEPTORS,), 0, FIN_DEV - 1), jax.random.fold_in(seeds[6], 1), 0, (FIN_DEV - 1) - 1).astype(jnp.int32)
    interp_weights = jnp.clip(1.0 * jax.random.uniform(seeds[7], (RECEPTORS, 2), jnp.float32) ** block_scale(seeds[7], (RECEPTORS, 2), ((0, 32),), -0.2, 0.2), 0.0, 1.0)
    return dict(section_state=section_state, base_state=base_state, axial_flow=axial_flow, fin_state=fin_state, receptor_rows=receptor_rows, donor_owner=donor_owner, donor_local=donor_local, interp_weights=interp_weights)


COURANT = 1.2
SECOND = 0.25
FOURTH = 0.03125
SECTION_WEIGHT = 0.6


def differences(extended, along, length):
    slices = [lax.slice_in_dim(extended, offset, offset + length, axis=along) for offset in range(5)]
    slope = 0.5 * (slices[3] - slices[1])
    fourth = slices[4] - 4.0 * slices[3] + 6.0 * slices[2] - 4.0 * slices[1] + slices[0]
    return slope, fourth


def section_rates(state, theta_ext, axial_ext, partner, flow, total_theta):
    radial = state.shape[3]
    spacing = 2.0 * math.pi / total_theta
    radius = jnp.arange(radial, dtype=jnp.float32) + 0.5
    mirror = jnp.array([1.0, -1.0, -1.0, 1.0], dtype=jnp.float32).reshape(4, 1, 1)
    pole_ghost = (partner * mirror)[..., None]
    far_ghost = jnp.zeros_like(pole_ghost)
    radial_ext = jnp.concatenate([pole_ghost, state, far_ghost], axis=3)
    upper_side = radial_ext[..., 2:]
    lower_side = radial_ext[..., :-2]
    radial_slope = 0.5 * (upper_side - lower_side)
    radial_second = upper_side - 2.0 * state + lower_side
    radius_ext = jnp.arange(radial + 2, dtype=jnp.float32) - 0.5
    moment = radial_ext[1] * radius_ext
    radial_div = 0.5 * (moment[..., 2:] - moment[..., :-2]) / radius
    theta_slope, theta_fourth = differences(theta_ext, 1, state.shape[1])
    axial_slope, axial_fourth = differences(axial_ext, 2, state.shape[2])
    inv_arc = 1.0 / (radius * spacing)
    spectral = flow + 2.0 + inv_arc
    advect = -flow * axial_slope
    pressure = advect[0] - (radial_div + theta_slope[2] * inv_arc + axial_slope[3])
    radial_vel = advect[1] - radial_slope[0]
    theta_vel = advect[2] - theta_slope[0] * inv_arc
    axial_vel = advect[3] - axial_slope[0]
    tendency = jnp.stack([pressure, radial_vel, theta_vel, axial_vel])
    damping = spectral * (SECOND * radial_second - FOURTH * (theta_fourth + axial_fourth))
    return (COURANT / spectral) * (tendency + damping)


def reference(section_state, base_state, axial_flow, fin_state, receptor_rows, donor_owner, donor_local, interp_weights):
    theta_ext = jnp.concatenate([section_state[:, -2:], section_state, section_state[:, :2]], axis=1)
    axial_ext = jnp.pad(section_state, ((0, 0), (0, 0), (2, 2), (0, 0)))
    partner = jnp.roll(section_state[..., 0], NTH // 2, axis=1)
    increment = section_rates(section_state, theta_ext, axial_ext, partner, axial_flow, NTH)
    section = base_state + SECTION_WEIGHT * increment
    device_of = jnp.arange(RECEPTORS, dtype=jnp.int32) // REC_DEV
    theta_cell = (device_of // N_AX) * TH_DEV + receptor_rows // Z_DEV
    axial_cell = (device_of % N_AX) * Z_DEV + receptor_rows % Z_DEV
    grid_rows = (theta_cell * NZ + axial_cell).astype(jnp.int32)
    donor = (donor_owner[:, 0] * FIN_DEV + donor_local).astype(jnp.int32)
    lower_row = fin_state[donor]
    upper_row = fin_state[donor + 1]
    fringe = interp_weights[:, 0, None, None] * lower_row + interp_weights[:, 1, None, None] * upper_row
    flat = section.reshape(COMPONENTS, NTH * NZ, NR)
    flat = flat.at[:, grid_rows, :].set(jnp.transpose(fringe, (1, 0, 2)))
    return flat.reshape(COMPONENTS, NTH, NZ, NR)
```

```python
import functools
import math

import jax
import jax.numpy as jnp
from jax import lax
from jax.experimental import pallas as pl
from jax.experimental.pallas import tpu as pltpu
from jax.sharding import PartitionSpec as P

COURANT = 1.2
SECOND = 0.25
FOURTH = 0.03125
SECTION_WEIGHT = 0.6

GAIN = SECTION_WEIGHT * COURANT
FOUR = GAIN * FOURTH
RAD = GAIN * SECOND
LANES = 128
PAD = 8
ANY = pl.BlockSpec(memory_space=pl.ANY)
VMEM = pl.BlockSpec(memory_space=pltpu.VMEM)
SMEM = pl.BlockSpec(memory_space=pltpu.SMEM)


def params(mib):
    return pltpu.CompilerParams(vmem_limit_bytes=mib * 2**20)


def cost(flops, moved):
    return pl.CostEstimate(flops=flops, bytes_accessed=moved, transcendentals=0)


def iota(shape, dim):
    return lax.broadcasted_iota(jnp.int32, shape, dim)


def theta_edges(state):
    comps, thetas, axials, radial = state.shape

    def kernel(s_ref, first_ref, last_ref, sems):
        one = pltpu.make_async_copy(s_ref.at[:, pl.ds(0, 2)], first_ref, sems.at[0])
        two = pltpu.make_async_copy(s_ref.at[:, pl.ds(thetas - 2, 2)], last_ref, sems.at[1])
        one.start()
        two.start()
        one.wait()
        two.wait()

    edge = jax.ShapeDtypeStruct((comps, 2, axials, radial), state.dtype)
    return pl.pallas_call(
        kernel,
        out_shape=(edge, edge),
        in_specs=[ANY],
        out_specs=(ANY, ANY),
        scratch_shapes=[pltpu.SemaphoreType.DMA((2,))],
        compiler_params=params(4),
        cost_estimate=cost(0, 4 * edge.size * 4),
        name="theta_edges",
    )(state)


def inner_edges(state):
    comps, thetas, axials, radial = state.shape
    step = 8
    width = max(LANES, -(-thetas // LANES) * LANES)

    def kernel(core_ref, low_ref, high_ref, first_ref, last_ref, pole_ref):
        t = pl.program_id(0)
        first_ref[...] = low_ref[:, :, 0:2, :]
        last_ref[...] = high_ref[:, :, 6:8, :]
        lane = iota((axials, width), 1)

        @pl.when(t == 0)
        def _():
            pole_ref[...] = jnp.zeros_like(pole_ref)

        for c in range(comps):
            held = pole_ref[c]
            for u in range(step):
                i = t * step + u
                column = jnp.broadcast_to(core_ref[c, u][:, 0:1], (axials, width))
                held = jnp.where(lane == i, column, held)
            pole_ref[c] = held

    edge = jax.ShapeDtypeStruct((comps, thetas, 2, radial), state.dtype)
    pole = jax.ShapeDtypeStruct((comps, axials, width), state.dtype)
    return pl.pallas_call(
        kernel,
        grid=(thetas // step,),
        in_specs=[
            pl.BlockSpec((comps, step, axials, LANES), lambda t: (0, t, 0, 0)),
            pl.BlockSpec((comps, step, 8, radial), lambda t: (0, t, 0, 0)),
            pl.BlockSpec((comps, step, 8, radial), lambda t: (0, t, axials // 8 - 1, 0)),
        ],
        out_specs=(
            pl.BlockSpec((comps, step, 2, radial), lambda t: (0, t, 0, 0)),
            pl.BlockSpec((comps, step, 2, radial), lambda t: (0, t, 0, 0)),
            pl.BlockSpec((comps, axials, width), lambda t: (0, 0, 0)),
        ),
        out_shape=(edge, edge, pole),
        compiler_params=params(32),
        cost_estimate=cost(state.size, 6 * 2**20),
        name="inner_edges",
    )(state, state, state)


def requests(owner, local, weights, n_az, n_ax, halves, my_half, cap, rows_dev):
    receptors = local.shape[0]
    half = n_ax // halves
    holders = n_az * half
    slots = halves * cap
    total = holders * slots
    width = -(-3 * slots // LANES) * LANES
    wide = max(total, width)

    def kernel(half_ref, owner_ref, local_ref, w_ref, table_ref, place_ref):
        square = (receptors, receptors)
        own_row = jnp.broadcast_to(owner_ref[...], square)
        down, across = iota(square, 0), iota(square, 1)
        same = down == across
        zero = jnp.zeros(square, jnp.int32)
        own_col = jnp.sum(jnp.where(same, own_row, zero), axis=1, keepdims=True)
        alike = own_row == own_col
        one = jnp.ones(square, jnp.int32)

        def place(own, rank):
            az, ax = own // n_ax, own % n_ax
            away = jnp.where(ax // half == half_ref[0], 0, 1) if halves > 1 else 0 * ax
            return (az * half + ax % half) * slots + away * cap + rank, away

        rank_row = jnp.sum(jnp.where(alike & (down < across), one, zero), axis=0, keepdims=True)
        rank_col = jnp.sum(jnp.where(alike & (across < down), one, zero), axis=1, keepdims=True)
        place_ref[...] = place(owner_ref[...], rank_row)[0]
        spot, away = place(own_col, rank_col)
        loc_row = jnp.broadcast_to(local_ref[...], square)
        line = jnp.sum(jnp.where(same, loc_row, zero), axis=1, keepdims=True) + away * rows_dev
        hit = iota((receptors, wide), 1) == spot
        fields = []
        for value in (line.astype(jnp.float32), w_ref[:, 0:1], w_ref[:, 1:2]):
            fields.append(jnp.sum(jnp.where(hit, value, 0.0), axis=0, keepdims=True))
        lane = iota((1, width), 1)
        for g in range(holders):
            packed = jnp.zeros((1, width), jnp.float32)
            for f, field in enumerate(fields):
                moved = pltpu.roll(field, (f * slots - g * slots) % wide, 1)[:, :width]
                packed = jnp.where(lane // slots == f, moved, packed)
            table_ref[g] = packed

    return pl.pallas_call(
        kernel,
        in_specs=[SMEM, VMEM, VMEM, VMEM],
        out_specs=(VMEM, VMEM),
        out_shape=(
            jax.ShapeDtypeStruct((holders, 1, width), jnp.float32),
            jax.ShapeDtypeStruct((1, receptors), jnp.int32),
        ),
        compiler_params=params(8),
        cost_estimate=cost(receptors * wide * 8, 2**17),
        name="requests",
    )(my_half, owner.reshape(1, receptors), local.reshape(1, receptors), weights)


def lines_of(fin):
    rows, comps, radial = fin.shape
    parts = radial // LANES
    return fin.reshape(rows, comps, parts, LANES).transpose(0, 2, 1, 3).reshape(rows * parts * comps, LANES)


def interpolate(table, blocks, slots, comps, radial):
    holders = table.shape[0]
    parts = radial // LANES
    line = comps * parts
    rows = blocks[0].shape[0]
    count = len(blocks)

    def kernel(*refs):
        t_ref, block_refs, out_ref, held = refs[0], refs[1 : 1 + count], refs[1 + count], refs[2 + count]
        per = rows // line
        for b, ref in enumerate(block_refs):
            for c in range(comps):
                for q in range(parts):
                    taken = ref[pl.ds(q * comps + c, per, stride=line), :]
                    held[pl.ds(b * rows + c * parts + q, per, stride=line), :] = taken

        def body(g, _):
            for s in range(slots):
                at = t_ref[g, s].astype(jnp.int32) * line
                at = pl.multiple_of(at, line)
                lower = held[pl.ds(at, line), :]
                upper = held[pl.ds(pl.multiple_of(at + line, line), line), :]
                out_ref[g * slots + s] = t_ref[g, slots + s] * lower + t_ref[g, 2 * slots + s] * upper
            return 0

        lax.fori_loop(0, holders, body, 0)

    return pl.pallas_call(
        kernel,
        in_specs=[SMEM] + [VMEM] * count,
        out_specs=VMEM,
        out_shape=jax.ShapeDtypeStruct((holders * slots, line, LANES), jnp.float32),
        scratch_shapes=[pltpu.VMEM((rows * count + line, LANES), jnp.float32)],
        compiler_params=params(8),
        cost_estimate=cost(holders * slots * line * LANES * 3, 2 * 2**20),
        name="interpolate",
    )(table, *blocks)


def radial_constants(radial, spacing, shape):
    j = iota(shape, len(shape) - 1).astype(jnp.float32)
    radius = j + 0.5
    inv_arc = 1.0 / (radius * spacing)
    return radius, inv_arc


def section_kernel(spacing, s_hbm, b_ref, w_ref, lo_ref, hi_ref, pole_ref, o_ref, held, sems):
    comps, rows, deep, radial = held.shape
    thetas = rows - 4
    axials = deep - 2 * PAD
    i = pl.program_id(0)

    def fetch(t):
        return pltpu.make_async_copy(
            s_hbm.at[:, t], held.at[:, t + 2, pl.ds(PAD, axials), :], sems.at[t]
        )

    @pl.when(i == 0)
    def _():
        for t in range(thetas):
            fetch(t).start()
        edge = jnp.zeros((axials, radial), jnp.float32)
        for c in range(comps):
            for t in (0, 1, rows - 2, rows - 1):
                held[c, t, PAD : PAD + axials, :] = edge
        for t in range(2):
            fetch(t).wait()

    @pl.when(i + 2 < thetas)
    def _():
        fetch(i + 2).wait()

    for c in range(comps):
        held[c, i + 2, PAD - 2 : PAD, :] = lo_ref[c, i]
        held[c, i + 2, PAD + axials : PAD + axials + 2, :] = hi_ref[c, i]

    size = min(axials, 32)
    shape = (size, radial)
    lane = iota(shape, 1)
    radius, inv_arc = radial_constants(radial, spacing, shape)
    outward = (radius + 1.0) / radius
    inward = (radius - 1.0) / radius
    signs = (1.0, -1.0, -1.0, 1.0)

    for k in range(0, axials, size):
        flow = w_ref[0, k : k + size, :]
        scale = (0.5 * GAIN) / (flow + 2.0 + inv_arc)
        at = PAD + k

        def here(c, t, shift=0):
            return held[c, i + 2 + t, at + shift : at + shift + size, :]

        smooth, ahead, tilt = [], [], []
        for c in range(comps):
            now = here(c, 0)
            a1p, a1m = here(c, 0, 1), here(c, 0, -1)
            t1p, t1m = here(c, 1), here(c, -1)
            inner = pltpu.roll(now, 1, 1)
            turned = pltpu.roll(pole_ref[c, k : k + size, :], pole_ref.shape[2] - i, 1)
            ghost = signs[c] * turned[:, 0:1]
            inner = jnp.where(lane == 0, ghost, inner)
            outer = jnp.where(lane == radial - 1, 0.0, pltpu.roll(now, radial - 1, 1))
            far = here(c, 2) + here(c, -2) + here(c, 0, 2) + here(c, 0, -2)
            near = t1p + t1m + a1p + a1m
            total = b_ref[c, 0, k : k + size, :] + RAD * (inner + outer)
            total = total + 4.0 * FOUR * near - FOUR * far - (2.0 * RAD + 12.0 * FOUR) * now
            smooth.append(total)
            ahead.append(a1p - a1m)
            if c == 0:
                p_theta = (t1p - t1m) * inv_arc
                p_radial = outer - inner
            elif c == 1:
                spread = outer * outward - inner * inward
            elif c == 2:
                t_theta = (t1p - t1m) * inv_arc
        gains = (
            spread + t_theta + ahead[3],
            p_radial,
            p_theta,
            ahead[0],
        )
        for c in range(comps):
            o_ref[c, 0, k : k + size, :] = smooth[c] - scale * (flow * ahead[c] + gains[c])


def section(state, base, flow, below, above, pole, spacing):
    comps, thetas, axials, radial = state.shape
    row = pl.BlockSpec((comps, 1, axials, radial), lambda i: (0, i, 0, 0))
    return pl.pallas_call(
        functools.partial(section_kernel, spacing),
        grid=(thetas,),
        in_specs=[
            ANY,
            row,
            pl.BlockSpec((1, axials, radial), lambda i: (i, 0, 0)),
            VMEM,
            VMEM,
            VMEM,
        ],
        out_specs=row,
        out_shape=jax.ShapeDtypeStruct(state.shape, state.dtype),
        scratch_shapes=[
            pltpu.VMEM((comps, thetas + 4, axials + 2 * PAD, radial), jnp.float32),
            pltpu.SemaphoreType.DMA((thetas,)),
        ],
        compiler_params=params(40),
        cost_estimate=cost(40 * state.size, 4 * (3 * state.size + flow.size)),
        name="section",
    )(state, base, flow, below, above, pole)


def theta_kernel(spacing, o_in, w_ref, lo_ref, hi_ref, o_ref):
    comps, two, axials, radial = o_in.shape
    side = pl.program_id(0)
    _, inv_arc = radial_constants(radial, spacing, (axials, radial))

    def add(edge, mate, near, far, sign):
        gain = sign * (0.5 * GAIN) * inv_arc / (w_ref[edge] + 2.0 + inv_arc)
        for c in range(comps):
            more = 4.0 * FOUR * near(c) - FOUR * far(c)
            if c == 0:
                more = more + gain * near(2)
            if c == 2:
                more = more + gain * near(0)
            o_ref[c, edge] = o_in[c, edge] + more
            o_ref[c, mate] = o_in[c, mate] - FOUR * near(c)

    @pl.when(side == 0)
    def _():
        add(0, 1, lambda c: lo_ref[c, 1], lambda c: lo_ref[c, 0], 1.0)

    @pl.when(side == 1)
    def _():
        add(1, 0, lambda c: hi_ref[c, 0], lambda c: hi_ref[c, 1], -1.0)


def theta_fix(out, flow, before, after, spacing):
    comps, thetas, axials, radial = out.shape
    last = thetas // 2 - 1
    rows = pl.BlockSpec((comps, 2, axials, radial), lambda s: (0, s * last, 0, 0))
    return pl.pallas_call(
        functools.partial(theta_kernel, spacing),
        grid=(2,),
        in_specs=[rows, pl.BlockSpec((2, axials, radial), lambda s: (s * last, 0, 0)), VMEM, VMEM],
        out_specs=rows,
        out_shape=jax.ShapeDtypeStruct(out.shape, out.dtype),
        input_output_aliases={0: 0},
        compiler_params=params(16),
        cost_estimate=cost(20 * before.size, 4 * 7 * before.size),
        name="theta_fix",
    )(out, flow, before, after)


def patch(out, lines, rows, place):
    comps, thetas, axials, radial = out.shape
    parts = radial // LANES
    count = rows.shape[0]
    tiles = thetas * axials // 8
    wide = out.reshape(comps, tiles, 8, parts, LANES).transpose(0, 1, 3, 2, 4)
    wide = wide.reshape(comps, tiles, parts, 8, 1, LANES)
    lines = lines.reshape(lines.shape[0], comps, parts, 1, LANES)

    def kernel(rows_ref, place_ref, lines_ref, _, o_ref, sem):
        def copy(n):
            row = rows_ref[n]
            return pltpu.make_async_copy(
                lines_ref.at[place_ref[n]], o_ref.at[:, row // 8, :, row % 8], sem
            )

        def start(n, _):
            copy(n).start()
            return 0

        lax.fori_loop(0, count, start, 0, unroll=4)
        pltpu.make_async_copy(
            lines_ref.at[pl.ds(0, count)], lines_ref.at[pl.ds(0, count)], sem
        ).wait()

    wide = pl.pallas_call(
        kernel,
        in_specs=[SMEM, SMEM, ANY, ANY],
        out_specs=ANY,
        out_shape=jax.ShapeDtypeStruct(wide.shape, wide.dtype),
        input_output_aliases={3: 0},
        scratch_shapes=[pltpu.SemaphoreType.DMA],
        compiler_params=params(4),
        cost_estimate=cost(0, 2 * count * comps * radial * 4),
        name="patch",
    )(rows, place, lines, wide)
    wide = wide.reshape(comps, tiles, parts, 8, LANES).transpose(0, 1, 3, 2, 4)
    return wide.reshape(out.shape)


def per_device(state, base, flow, fin, receptor_rows, donor_owner, donor_local, weights):
    comps, thetas, axials, radial = state.shape
    n_az, n_ax = lax.axis_size("az"), lax.axis_size("ax")
    devices = n_az * n_ax
    receptors = receptor_rows.shape[0]
    cap = max(2, 2 * receptors // devices)
    halves = 2 if n_ax % 2 == 0 else 1
    half = n_ax // halves
    spacing = 2.0 * math.pi / (thetas * n_az)
    both = ("az", "ax")
    groups = [
        [a * n_ax + h * half + q for a in range(n_az) for q in range(half)] for h in range(halves)
    ]
    my_half = (lax.axis_index("ax") // half).reshape(1).astype(jnp.int32)

    def exchange(x):
        return lax.all_to_all(x, both, 0, 0, axis_index_groups=groups, tiled=True)

    def around(x, by):
        return lax.ppermute(x, "az", [(a, (a + by) % n_az) for a in range(n_az)])

    def along(x, by):
        return lax.ppermute(x, "ax", [(a, a + by) for a in range(n_ax) if 0 <= a + by < n_ax])

    blocks = [fin]
    if halves == 2:
        blocks.append(lax.ppermute(fin, "ax", [(a, (a + half) % n_ax) for a in range(n_ax)]))
    table, place = requests(
        donor_owner[:, 0], donor_local, weights, n_az, n_ax, halves, my_half, cap, fin.shape[0]
    )
    first, last = theta_edges(state)
    before, after = around(last, 1), around(first, -1)
    asked = exchange(table)
    low, high, pole = inner_edges(state)
    below, above = along(high, 1), along(low, -1)
    pole = around(pole, n_az // 2)

    lines = interpolate(
        asked.reshape(asked.shape[0], -1), [lines_of(b) for b in blocks], halves * cap, comps, radial
    )
    lines = exchange(lines)
    out = section(state, base, flow, below, above, pole, spacing)
    out = theta_fix(out, flow, before, after, spacing)
    return patch(out, lines, receptor_rows, place.reshape(receptors))


def solution(mesh):
    placed = (
        P(None, "az", "ax", None),
        P(None, "az", "ax", None),
        P("az", "ax", None),
        P(("az", "ax"), None, None),
        P(("az", "ax")),
        P(("az", "ax"), None),
        P(("az", "ax")),
        P(("az", "ax"), None),
    )
    return jax.shard_map(
        per_device, mesh=mesh, in_specs=placed, out_specs=P(None, "az", "ax", None), check_vma=False
    )
```

```python
import functools
import math

import jax
import jax.numpy as jnp
from jax import lax
from jax.experimental import pallas as pl
from jax.experimental.pallas import tpu as pltpu
from jax.sharding import PartitionSpec as P

COURANT = 1.2
SECOND = 0.25
FOURTH = 0.03125
SECTION_WEIGHT = 0.6

GAIN = SECTION_WEIGHT * COURANT
FOUR = GAIN * FOURTH
RAD = GAIN * SECOND
LANES = 128
PAD = 8
ANY = pl.BlockSpec(memory_space=pl.ANY)
HBM = pl.BlockSpec(memory_space=pltpu.HBM)
VMEM = pl.BlockSpec(memory_space=pltpu.VMEM)
SMEM = pl.BlockSpec(memory_space=pltpu.SMEM)


def params(mib):
    return pltpu.CompilerParams(vmem_limit_bytes=mib * 2**20)


def cost(flops, moved):
    return pl.CostEstimate(flops=flops // 1000, bytes_accessed=moved // 1000, transcendentals=0)


def iota(shape, dim):
    return lax.broadcasted_iota(jnp.int32, shape, dim)


def theta_edges(state):
    comps, thetas, axials, radial = state.shape

    def kernel(low_ref, high_ref, first_ref, last_ref):
        first_ref[...] = low_ref[...]
        last_ref[...] = high_ref[...]

    def pair(at):
        return pl.BlockSpec((1, 2, axials, radial), lambda c: (c, at, 0, 0))

    edge = jax.ShapeDtypeStruct((comps, 2, axials, radial), state.dtype)
    return pl.pallas_call(
        kernel,
        grid=(comps,),
        in_specs=[pair(0), pair(thetas // 2 - 1)],
        out_specs=(pair(0), pair(0)),
        out_shape=(edge, edge),
        compiler_params=params(60),
        cost_estimate=cost(0, 4 * edge.size * 4),
        name="theta_edges",
    )(state, state)


def inner_edges(state):
    comps, thetas, axials, radial = state.shape
    step = 4
    width = max(LANES, -(-thetas // LANES) * LANES)

    def kernel(core_ref, first_ref, last_ref, pole_ref):
        t = pl.program_id(0)
        first_ref[...] = core_ref[:, :, 0:2, :]
        last_ref[...] = core_ref[:, :, axials - 2 : axials, :]
        lane = iota((axials, width), 1)

        @pl.when(t == 0)
        def _():
            pole_ref[...] = jnp.zeros_like(pole_ref)

        for c in range(comps):
            held = pole_ref[c]
            for u in range(step):
                i = t * step + u
                column = jnp.broadcast_to(core_ref[c, u][:, 0:1], (axials, width))
                held = jnp.where(lane == i, column, held)
            pole_ref[c] = held

    edge = jax.ShapeDtypeStruct((comps, thetas, 2, radial), state.dtype)
    pole = jax.ShapeDtypeStruct((comps, axials, width), state.dtype)
    return pl.pallas_call(
        kernel,
        grid=(thetas // step,),
        in_specs=[pl.BlockSpec((comps, step, axials, radial), lambda t: (0, t, 0, 0))],
        out_specs=(
            pl.BlockSpec((comps, step, 2, radial), lambda t: (0, t, 0, 0)),
            pl.BlockSpec((comps, step, 2, radial), lambda t: (0, t, 0, 0)),
            pl.BlockSpec((comps, axials, width), lambda t: (0, 0, 0)),
        ),
        out_shape=(edge, edge, pole),
        compiler_params=params(60),
        cost_estimate=cost(state.size, 6 * 2**20),
        name="inner_edges",
    )(state)


def requests(owner, local, weights, n_az, n_ax, halves, my_half, cap, rows_dev):
    receptors = local.shape[0]
    half = n_ax // halves
    holders = n_az * half
    slots = halves * cap
    total = holders * slots
    width = -(-3 * slots // LANES) * LANES
    wide = max(total, width)

    def kernel(half_ref, owner_ref, local_ref, w_ref, table_ref, place_ref):
        square = (receptors, receptors)
        own_row = jnp.broadcast_to(owner_ref[...], square)
        down, across = iota(square, 0), iota(square, 1)
        same = down == across
        zero = jnp.zeros(square, jnp.int32)
        own_col = jnp.sum(jnp.where(same, own_row, zero), axis=1, keepdims=True)
        alike = own_row == own_col
        one = jnp.ones(square, jnp.int32)

        def place(own, rank):
            az, ax = own // n_ax, own % n_ax
            away = jnp.where(ax // half == half_ref[0], 0, 1) if halves > 1 else 0 * ax
            return (az * half + ax % half) * slots + away * cap + rank, away

        rank_row = jnp.sum(jnp.where(alike & (down < across), one, zero), axis=0, keepdims=True)
        rank_col = jnp.sum(jnp.where(alike & (across < down), one, zero), axis=1, keepdims=True)
        place_ref[...] = place(owner_ref[...], rank_row)[0]
        spot, away = place(own_col, rank_col)
        loc_row = jnp.broadcast_to(local_ref[...], square)
        line = jnp.sum(jnp.where(same, loc_row, zero), axis=1, keepdims=True) + away * rows_dev
        hit = iota((receptors, wide), 1) == spot
        fields = []
        for value in (line.astype(jnp.float32), w_ref[:, 0:1], w_ref[:, 1:2]):
            fields.append(jnp.sum(jnp.where(hit, value, 0.0), axis=0, keepdims=True))
        lane = iota((1, width), 1)
        for g in range(holders):
            packed = jnp.zeros((1, width), jnp.float32)
            for f, field in enumerate(fields):
                moved = pltpu.roll(field, (f * slots - g * slots) % wide, 1)[:, :width]
                packed = jnp.where(lane // slots == f, moved, packed)
            table_ref[g] = packed

    return pl.pallas_call(
        kernel,
        in_specs=[SMEM, VMEM, VMEM, VMEM],
        out_specs=(VMEM, VMEM),
        out_shape=(
            jax.ShapeDtypeStruct((holders, 1, width), jnp.float32),
            jax.ShapeDtypeStruct((1, receptors), jnp.int32),
        ),
        compiler_params=params(8),
        cost_estimate=cost(receptors * wide * 8, 2**17),
        name="requests",
    )(my_half, owner.reshape(1, receptors), local.reshape(1, receptors), weights)


def lines_of(fin):
    rows, comps, radial = fin.shape
    parts = radial // LANES
    return fin.reshape(rows, comps, parts, LANES).transpose(0, 2, 1, 3).reshape(rows * parts * comps, LANES)


def interpolate(table, blocks, slots, comps, radial):
    holders = table.shape[0]
    parts = radial // LANES
    line = comps * parts
    rows = blocks[0].shape[0]
    count = len(blocks)

    def kernel(*refs):
        t_ref, block_refs, out_ref, held = refs[0], refs[1 : 1 + count], refs[1 + count], refs[2 + count]
        per = rows // line
        for b, ref in enumerate(block_refs):
            for c in range(comps):
                for q in range(parts):
                    taken = ref[pl.ds(q * comps + c, per, stride=line), :]
                    held[pl.ds(b * rows + c * parts + q, per, stride=line), :] = taken

        def body(g, _):
            for s in range(slots):
                at = t_ref[g, s].astype(jnp.int32) * line
                at = pl.multiple_of(at, line)
                lower = held[pl.ds(at, line), :]
                upper = held[pl.ds(pl.multiple_of(at + line, line), line), :]
                out_ref[g * slots + s] = t_ref[g, slots + s] * lower + t_ref[g, 2 * slots + s] * upper
            return 0

        lax.fori_loop(0, holders, body, 0)

    return pl.pallas_call(
        kernel,
        in_specs=[SMEM] + [VMEM] * count,
        out_specs=VMEM,
        out_shape=jax.ShapeDtypeStruct((holders * slots, line, LANES), jnp.float32),
        scratch_shapes=[pltpu.VMEM((rows * count + line, LANES), jnp.float32)],
        compiler_params=params(8),
        cost_estimate=cost(holders * slots * line * LANES * 3, 2 * 2**20),
        name="interpolate",
    )(table, *blocks)


def radial_constants(radial, spacing, shape):
    j = iota(shape, len(shape) - 1).astype(jnp.float32)
    radius = j + 0.5
    inv_arc = 1.0 / (radius * spacing)
    return radius, inv_arc


def section_kernel(spacing, s_hbm, b_hbm, w_hbm, lo_ref, hi_ref, pole_ref, o_hbm, held, work, flows, sems):
    comps, rows, deep, radial = held.shape
    thetas = rows - 4
    axials = deep - 2 * PAD

    def copy_in(t, which):
        if which == 0:
            source, target = s_hbm.at[:, t], held.at[:, t + 2, pl.ds(PAD, axials), :]
        elif which == 1:
            source, target = b_hbm.at[:, t], work.at[:, t]
        else:
            source, target = w_hbm.at[t], flows.at[t]
        return pltpu.make_async_copy(source, target, sems.at[which, t])

    def store(t):
        return pltpu.make_async_copy(work.at[:, t], o_hbm.at[:, t], sems.at[3, t])

    for t in range(thetas):
        for which in range(3):
            copy_in(t, which).start()
    edge = jnp.zeros((axials, radial), jnp.float32)
    for c in range(comps):
        for t in (0, 1, rows - 2, rows - 1):
            held[c, t, PAD : PAD + axials, :] = edge
    for t in range(2):
        copy_in(t, 0).wait()

    def row(i, _):
        section_row(i, spacing, copy_in, lo_ref, hi_ref, pole_ref, held, work, flows)
        store(i).start()
        return 0

    lax.fori_loop(0, thetas, row, 0)

    def drain(i, _):
        store(i).wait()
        return 0

    lax.fori_loop(0, thetas, drain, 0)


def section_row(i, spacing, copy_in, lo_ref, hi_ref, pole_ref, held, work, flows):
    comps, rows, deep, radial = held.shape
    thetas = rows - 4
    axials = deep - 2 * PAD

    @pl.when(i + 2 < thetas)
    def _():
        copy_in(i + 2, 0).wait()

    copy_in(i, 1).wait()
    copy_in(i, 2).wait()
    for c in range(comps):
        held[c, i + 2, PAD - 2 : PAD, :] = lo_ref[c, i]
        held[c, i + 2, PAD + axials : PAD + axials + 2, :] = hi_ref[c, i]

    size = min(axials, 32)
    shape = (size, radial)
    lane = iota(shape, 1)
    radius, inv_arc = radial_constants(radial, spacing, shape)
    outward = (radius + 1.0) / radius
    inward = (radius - 1.0) / radius
    signs = (1.0, -1.0, -1.0, 1.0)

    for k in range(0, axials, size):
        flow = flows[i, k : k + size, :]
        scale = (0.5 * GAIN) / (flow + 2.0 + inv_arc)
        at = PAD + k

        def here(c, t, shift=0):
            return held[c, i + 2 + t, at + shift : at + shift + size, :]

        smooth, ahead, tilt = [], [], []
        for c in range(comps):
            now = here(c, 0)
            a1p, a1m = here(c, 0, 1), here(c, 0, -1)
            t1p, t1m = here(c, 1), here(c, -1)
            ghost = pltpu.roll(pole_ref[c, k : k + size, :], pole_ref.shape[2] - i, 1)
            if signs[c] < 0:
                ghost = -ghost
            inner = pltpu.roll(now, 1, 1)
            inner = jnp.concatenate(
                [jnp.where(lane[:, :LANES] == 0, ghost, inner[:, :LANES]), inner[:, LANES:]], axis=1
            )
            outer = jnp.where(lane == radial - 1, 0.0, pltpu.roll(now, radial - 1, 1))
            far = here(c, 2) + here(c, -2) + here(c, 0, 2) + here(c, 0, -2)
            near = t1p + t1m + a1p + a1m
            total = work[c, i, k : k + size, :] + RAD * (inner + outer)
            total = total + 4.0 * FOUR * near - FOUR * far - (2.0 * RAD + 12.0 * FOUR) * now
            smooth.append(total)
            ahead.append(a1p - a1m)
            if c == 0:
                p_theta = (t1p - t1m) * inv_arc
                p_radial = outer - inner
            elif c == 1:
                spread = outer * outward - inner * inward
            elif c == 2:
                t_theta = (t1p - t1m) * inv_arc
        gains = (
            spread + t_theta + ahead[3],
            p_radial,
            p_theta,
            ahead[0],
        )
        for c in range(comps):
            work[c, i, k : k + size, :] = smooth[c] - scale * (flow * ahead[c] + gains[c])


def section(state, base, flow, below, above, pole, spacing):
    comps, thetas, axials, radial = state.shape
    return pl.pallas_call(
        functools.partial(section_kernel, spacing),
        in_specs=[HBM, HBM, HBM, VMEM, VMEM, VMEM],
        out_specs=HBM,
        out_shape=jax.ShapeDtypeStruct(state.shape, state.dtype),
        scratch_shapes=[
            pltpu.VMEM((comps, thetas + 4, axials + 2 * PAD, radial), jnp.float32),
            pltpu.VMEM(state.shape, jnp.float32),
            pltpu.VMEM(flow.shape, jnp.float32),
            pltpu.SemaphoreType.DMA((4, thetas)),
        ],
        compiler_params=params(60),
        cost_estimate=cost(40 * state.size, 4 * (3 * state.size + flow.size)),
        name="section",
    )(state, base, flow, below, above, pole)


def theta_kernel(spacing, o_in, w_ref, lo_ref, hi_ref, o_ref):
    comps, two, axials, radial = o_in.shape
    side = pl.program_id(0)
    _, inv_arc = radial_constants(radial, spacing, (axials, radial))

    def add(edge, mate, near, far, sign):
        gain = sign * (0.5 * GAIN) * inv_arc / (w_ref[edge] + 2.0 + inv_arc)
        for c in range(comps):
            more = 4.0 * FOUR * near(c) - FOUR * far(c)
            if c == 0:
                more = more + gain * near(2)
            if c == 2:
                more = more + gain * near(0)
            o_ref[c, edge] = o_in[c, edge] + more
            o_ref[c, mate] = o_in[c, mate] - FOUR * near(c)

    @pl.when(side == 0)
    def _():
        add(0, 1, lambda c: lo_ref[c, 1], lambda c: lo_ref[c, 0], 1.0)

    @pl.when(side == 1)
    def _():
        add(1, 0, lambda c: hi_ref[c, 0], lambda c: hi_ref[c, 1], -1.0)


def theta_fix(out, flow, before, after, spacing):
    comps, thetas, axials, radial = out.shape
    last = thetas // 2 - 1
    rows = pl.BlockSpec((comps, 2, axials, radial), lambda s: (0, s * last, 0, 0))
    return pl.pallas_call(
        functools.partial(theta_kernel, spacing),
        grid=(2,),
        in_specs=[rows, pl.BlockSpec((2, axials, radial), lambda s: (s * last, 0, 0)), VMEM, VMEM],
        out_specs=rows,
        out_shape=jax.ShapeDtypeStruct(out.shape, out.dtype),
        input_output_aliases={0: 0},
        compiler_params=params(16),
        cost_estimate=cost(20 * before.size, 4 * 7 * before.size),
        name="theta_fix",
    )(out, flow, before, after)


def patch(out, lines, rows, place):
    comps, thetas, axials, radial = out.shape
    parts = radial // LANES
    count = rows.shape[0]
    tiles = thetas * axials // 8
    wide = out.reshape(comps, tiles, 8, parts, LANES).transpose(0, 1, 3, 2, 4)
    wide = wide.reshape(comps, tiles, parts, 8, 1, LANES)
    lines = lines.reshape(lines.shape[0], comps, parts, 1, LANES)

    def kernel(rows_ref, place_ref, lines_ref, _, o_ref, sem):
        def copy(n):
            row = rows_ref[n]
            return pltpu.make_async_copy(
                lines_ref.at[place_ref[n]], o_ref.at[:, row // 8, :, row % 8], sem
            )

        def start(n, _):
            copy(n).start()
            return 0

        lax.fori_loop(0, count, start, 0, unroll=4)
        pltpu.make_async_copy(
            lines_ref.at[pl.ds(0, count)], lines_ref.at[pl.ds(0, count)], sem
        ).wait()

    wide = pl.pallas_call(
        kernel,
        in_specs=[SMEM, SMEM, ANY, HBM],
        out_specs=HBM,
        out_shape=jax.ShapeDtypeStruct(wide.shape, wide.dtype),
        input_output_aliases={3: 0},
        scratch_shapes=[pltpu.SemaphoreType.DMA],
        compiler_params=params(4),
        cost_estimate=cost(0, 2 * count * comps * radial * 4),
        name="patch",
    )(rows, place, lines, wide)
    wide = wide.reshape(comps, tiles, parts, 8, LANES).transpose(0, 1, 3, 2, 4)
    return wide.reshape(out.shape)


def behind(value, done):
    return lax.optimization_barrier((value, done))


def per_device(state, base, flow, fin, receptor_rows, donor_owner, donor_local, weights):
    comps, thetas, axials, radial = state.shape
    n_az, n_ax = lax.axis_size("az"), lax.axis_size("ax")
    devices = n_az * n_ax
    receptors = receptor_rows.shape[0]
    cap = max(2, 2 * receptors // devices)
    halves = 2 if n_ax % 2 == 0 else 1
    half = n_ax // halves
    spacing = 2.0 * math.pi / (thetas * n_az)
    both = ("az", "ax")
    groups = [
        [a * n_ax + h * half + q for a in range(n_az) for q in range(half)] for h in range(halves)
    ]
    my_half = (lax.axis_index("ax") // half).reshape(1).astype(jnp.int32)

    def exchange(x):
        return lax.all_to_all(x, both, 0, 0, axis_index_groups=groups, tiled=True)

    def around(x, by):
        return lax.ppermute(x, "az", [(a, (a + by) % n_az) for a in range(n_az)])

    def along(x, by):
        return lax.ppermute(x, "ax", [(a, a + by) for a in range(n_ax) if 0 <= a + by < n_ax])

    blocks = [fin]
    if halves == 2:
        blocks.append(lax.ppermute(fin, "ax", [(a, (a + half) % n_ax) for a in range(n_ax)]))
    first, last = theta_edges(state)
    before, after = around(last, 1), around(first, -1)
    owner, first = behind(donor_owner[:, 0], first)
    table, place = requests(
        owner, donor_local, weights, n_az, n_ax, halves, my_half, cap, fin.shape[0]
    )
    asked = exchange(table)
    later, table = behind(state, table)
    low, high, pole = inner_edges(later)
    below, above = along(high, 1), along(low, -1)
    asked, low = behind(asked, low)
    pole = around(pole, n_az // 2)
    lines = interpolate(
        asked.reshape(asked.shape[0], -1), [lines_of(b) for b in blocks], halves * cap, comps, radial
    )
    lines, before, after, below, above, pole = lax.optimization_barrier(
        (lines, before, after, below, above, pole)
    )
    base, lines = behind(base, lines)
    lines = exchange(lines)
    out = section(state, base, flow, below, above, pole, spacing)
    out = theta_fix(out, flow, before, after, spacing)
    return patch(out, lines, receptor_rows, place.reshape(receptors))


def solution(mesh):
    placed = (
        P(None, "az", "ax", None),
        P(None, "az", "ax", None),
        P("az", "ax", None),
        P(("az", "ax"), None, None),
        P(("az", "ax")),
        P(("az", "ax"), None),
        P(("az", "ax")),
        P(("az", "ax"), None),
    )
    return jax.shard_map(
        per_device, mesh=mesh, in_specs=placed, out_specs=P(None, "az", "ax", None), check_vma=False
    )
```

```python
import functools
import math

import jax
import jax.numpy as jnp
from jax import lax
from jax.experimental import pallas as pl
from jax.experimental.pallas import tpu as pltpu
from jax.sharding import PartitionSpec as P

COURANT = 1.2
SECOND = 0.25
FOURTH = 0.03125
SECTION_WEIGHT = 0.6

GAIN = SECTION_WEIGHT * COURANT
FOUR = GAIN * FOURTH
RAD = GAIN * SECOND
LANES = 128
PAD = 8
GROUP = 2
AHEAD = 5
TALL = 20
ANY = pl.BlockSpec(memory_space=pl.ANY)
HBM = pl.BlockSpec(memory_space=pltpu.HBM)
VMEM = pl.BlockSpec(memory_space=pltpu.VMEM)
SMEM = pl.BlockSpec(memory_space=pltpu.SMEM)


def params(mib):
    return pltpu.CompilerParams(vmem_limit_bytes=mib * 2**20)


def cost(flops, moved):
    return pl.CostEstimate(flops=flops // 1000, bytes_accessed=moved // 1000, transcendentals=0)


def iota(shape, dim):
    return lax.broadcasted_iota(jnp.int32, shape, dim)


def theta_edges(state):
    comps, thetas, axials, radial = state.shape

    def kernel(s_ref, first_ref, last_ref, held, sems):
        def copies(n):
            side, c = n % 2, n // 2
            at, out = ((0, first_ref), (thetas - 2, last_ref))[side]
            return (
                pltpu.make_async_copy(s_ref.at[c, pl.ds(at, 2)], held.at[n], sems.at[0, n]),
                pltpu.make_async_copy(held.at[n], out.at[c], sems.at[1, n]),
            )

        moves = [copies(n) for n in range(2 * comps)]
        for come, _ in moves:
            come.start()
        for come, go in moves:
            come.wait()
            go.start()
        for _, go in moves:
            go.wait()

    edge = jax.ShapeDtypeStruct((comps, 2, axials, radial), state.dtype)
    return pl.pallas_call(
        kernel,
        in_specs=[HBM],
        out_specs=(HBM, HBM),
        out_shape=(edge, edge),
        scratch_shapes=[
            pltpu.VMEM((2 * comps, 2, axials, radial), jnp.float32),
            pltpu.SemaphoreType.DMA((2, 2 * comps)),
        ],
        compiler_params=params(60),
        cost_estimate=cost(0, 4 * edge.size * 4),
        name="theta_edges",
    )(state)


def pole_fold(thetas, axials):
    fold = LANES // thetas if LANES % thetas == 0 else 1
    while fold > 1 and axials % (8 * fold):
        fold //= 2
    return fold


def inner_edges(state):
    comps, thetas, axials, radial = state.shape
    fold = pole_fold(thetas, axials)
    part = axials // fold
    width = max(LANES, -(-thetas // LANES) * LANES)
    group = 4

    def kernel(s_ref, first_ref, last_ref, pole_ref, core, low, high, sems):
        def core_copy(t):
            return pltpu.make_async_copy(
                s_ref.at[:, t, :, pl.ds(0, LANES)], core.at[:, t], sems.at[0, t]
            )

        def edge_copy(g, at, out, n):
            rows = pl.ds(g * group, group)
            return pltpu.make_async_copy(
                s_ref.at[:, rows, pl.ds(at, 8), :], out.at[:, rows], sems.at[n, g]
            )

        for t in range(thetas):
            core_copy(t).start()
            if t % group == 0:
                edge_copy(t // group, 0, low, 1).start()
                edge_copy(t // group, axials - 8, high, 2).start()
        lane = iota((part, width), 1)
        pole_ref[...] = jnp.zeros_like(pole_ref)

        def body(g, _):
            for u in range(group):
                core_copy(g * group + u).wait()
            edge_copy(g, 0, low, 1).wait()
            edge_copy(g, axials - 8, high, 2).wait()
            for u in range(group):
                i = g * group + u
                for c in range(comps):
                    first_ref[c, i] = low[c, i, 0:2, :]
                    last_ref[c, i] = high[c, i, 6:8, :]
            for c in range(comps):
                packed = pole_ref[c]
                for u in range(group):
                    i = g * group + u
                    for f in range(fold):
                        column = core[c, i, f * part : (f + 1) * part, 0:1]
                        column = jnp.broadcast_to(column, (part, width))
                        packed = jnp.where(lane == i + f * thetas, column, packed)
                pole_ref[c] = packed
            return 0

        lax.fori_loop(0, thetas // group, body, 0)

    edge = jax.ShapeDtypeStruct((comps, thetas, 2, radial), state.dtype)
    pole = jax.ShapeDtypeStruct((comps, part, width), state.dtype)
    return pl.pallas_call(
        kernel,
        in_specs=[HBM],
        out_specs=(VMEM, VMEM, VMEM),
        out_shape=(edge, edge, pole),
        scratch_shapes=[
            pltpu.VMEM((comps, thetas, axials, LANES), jnp.float32),
            pltpu.VMEM((comps, thetas, 8, radial), jnp.float32),
            pltpu.VMEM((comps, thetas, 8, radial), jnp.float32),
            pltpu.SemaphoreType.DMA((3, thetas)),
        ],
        compiler_params=params(60),
        cost_estimate=cost(state.size, 6 * 2**20),
        name="inner_edges",
    )(state)


def requests(owner, local, weights, n_az, n_ax, halves, my_half, cap, rows_dev):
    receptors = local.shape[0]
    half = n_ax // halves
    holders = n_az * half
    slots = halves * cap
    total = holders * slots
    width = -(-3 * slots // LANES) * LANES
    wide = max(total, width)

    def kernel(half_ref, owner_ref, local_ref, w_ref, table_ref, place_ref):
        square = (receptors, receptors)
        own_row = jnp.broadcast_to(owner_ref[...], square)
        down, across = iota(square, 0), iota(square, 1)
        same = down == across
        zero = jnp.zeros(square, jnp.int32)
        own_col = jnp.sum(jnp.where(same, own_row, zero), axis=1, keepdims=True)
        alike = own_row == own_col
        one = jnp.ones(square, jnp.int32)

        def place(own, rank):
            az, ax = own // n_ax, own % n_ax
            away = jnp.where(ax // half == half_ref[0], 0, 1) if halves > 1 else 0 * ax
            return (az * half + ax % half) * slots + away * cap + rank, away

        rank_row = jnp.sum(jnp.where(alike & (down < across), one, zero), axis=0, keepdims=True)
        rank_col = jnp.sum(jnp.where(alike & (across < down), one, zero), axis=1, keepdims=True)
        place_ref[...] = place(owner_ref[...], rank_row)[0]
        spot, away = place(own_col, rank_col)
        loc_row = jnp.broadcast_to(local_ref[...], square)
        line = jnp.sum(jnp.where(same, loc_row, zero), axis=1, keepdims=True) + away * rows_dev
        hit = iota((receptors, wide), 1) == spot
        fields = []
        for value in (line.astype(jnp.float32), w_ref[:, 0:1], w_ref[:, 1:2]):
            fields.append(jnp.sum(jnp.where(hit, value, 0.0), axis=0, keepdims=True))
        lane = iota((1, width), 1)
        for g in range(holders):
            packed = jnp.zeros((1, width), jnp.float32)
            for f, field in enumerate(fields):
                moved = pltpu.roll(field, (f * slots - g * slots) % wide, 1)[:, :width]
                packed = jnp.where(lane // slots == f, moved, packed)
            table_ref[g] = jnp.broadcast_to(packed, (TALL, width))

    return pl.pallas_call(
        kernel,
        in_specs=[SMEM, VMEM, VMEM, VMEM],
        out_specs=(VMEM, VMEM),
        out_shape=(
            jax.ShapeDtypeStruct((holders, TALL, width), jnp.float32),
            jax.ShapeDtypeStruct((1, receptors), jnp.int32),
        ),
        compiler_params=params(8),
        cost_estimate=cost(receptors * wide * 8, 2**17),
        name="requests",
    )(my_half, owner.reshape(1, receptors), local.reshape(1, receptors), weights)


def lines_of(fin):
    rows, comps, radial = fin.shape
    parts = radial // LANES
    return fin.reshape(rows, comps, parts, LANES).transpose(0, 2, 1, 3).reshape(rows * parts * comps, LANES)


def interpolate(table, blocks, slots, comps, radial):
    holders = table.shape[0]
    parts = radial // LANES
    line = comps * parts
    rows = blocks[0].shape[0]
    count = len(blocks)

    def kernel(*refs):
        t_ref, block_refs, out_ref, held = refs[0], refs[1 : 1 + count], refs[1 + count], refs[2 + count]
        per = rows // line
        for b, ref in enumerate(block_refs):
            for c in range(comps):
                for q in range(parts):
                    taken = ref[pl.ds(q * comps + c, per, stride=line), :]
                    held[pl.ds(b * rows + c * parts + q, per, stride=line), :] = taken

        def body(g, _):
            for s in range(slots):
                at = t_ref[g, s].astype(jnp.int32) * line
                at = pl.multiple_of(at, line)
                lower = held[pl.ds(at, line), :]
                upper = held[pl.ds(pl.multiple_of(at + line, line), line), :]
                out_ref[g * slots + s] = t_ref[g, slots + s] * lower + t_ref[g, 2 * slots + s] * upper
            return 0

        lax.fori_loop(0, holders, body, 0)

    return pl.pallas_call(
        kernel,
        in_specs=[SMEM] + [VMEM] * count,
        out_specs=VMEM,
        out_shape=jax.ShapeDtypeStruct((holders * slots, line, LANES), jnp.float32),
        scratch_shapes=[pltpu.VMEM((rows * count + line, LANES), jnp.float32)],
        compiler_params=params(8),
        cost_estimate=cost(holders * slots * line * LANES * 3, 2 * 2**20),
        name="interpolate",
    )(table, *blocks)


def radial_constants(radial, spacing, shape):
    j = iota(shape, len(shape) - 1).astype(jnp.float32)
    radius = j + 0.5
    inv_arc = 1.0 / (radius * spacing)
    return radius, inv_arc


def section_kernel(spacing, *refs):
    s_hbm, b_hbm, w_hbm, before, after, lo_ref, hi_ref, pole_ref, o_hbm, held, work, flows, sems = refs
    comps, rows, deep, radial = held.shape
    thetas = rows - 4
    axials = deep - 2 * PAD
    groups = thetas // GROUP
    inside = pl.ds(PAD, axials)

    def copy_in(g, which):
        some = pl.ds(g * GROUP, GROUP)
        if which == 0:
            source, target = s_hbm.at[:, some], held.at[:, pl.ds(g * GROUP + 2, GROUP), inside, :]
        elif which == 1:
            source, target = b_hbm.at[:, some], work.at[:, some]
        else:
            source, target = w_hbm.at[some], flows.at[some]
        return pltpu.make_async_copy(source, target, sems.at[which, g])

    def store(g):
        some = pl.ds(g * GROUP, GROUP)
        return pltpu.make_async_copy(work.at[:, some], o_hbm.at[:, some], sems.at[3, g])

    def halo(side):
        source, at = ((before, 0), (after, rows - 2))[side]
        return pltpu.make_async_copy(source, held.at[:, pl.ds(at, 2), inside, :], sems.at[4, side])

    def begin(g):
        for which in range(3):
            copy_in(g, which).start()

    halo(0).start()
    for g in range(min(AHEAD, groups)):
        begin(g)
    halo(1).start()
    halo(0).wait()
    copy_in(0, 0).wait()

    def step(g, _):
        @pl.when(g + AHEAD < groups)
        def _():
            begin(g + AHEAD)

        @pl.when(g + 1 < groups)
        def _():
            copy_in(g + 1, 0).wait()

        @pl.when(g + 1 == groups)
        def _():
            halo(1).wait()

        copy_in(g, 1).wait()
        copy_in(g, 2).wait()
        for u in range(GROUP):
            section_row(g * GROUP + u, spacing, lo_ref, hi_ref, pole_ref, held, work, flows)
        store(g).start()
        return 0

    lax.fori_loop(0, groups, step, 0)

    def drain(g, _):
        store(g).wait()
        return 0

    lax.fori_loop(0, groups, drain, 0)


def pole_ghost(pole_ref, c, k, size, i, thetas):
    part, width = pole_ref.shape[1:]
    pieces = []
    while size > 0:
        f, at = k // part, k % part
        take = min(size, part - at)
        piece = pole_ref[c, at : at + take, :]
        pieces.append(pltpu.roll(piece, width - i - f * thetas, 1)[:, :LANES])
        k, size = k + take, size - take
    return jnp.concatenate(pieces, axis=0) if len(pieces) > 1 else pieces[0]


def section_row(i, spacing, lo_ref, hi_ref, pole_ref, held, work, flows):
    comps, rows, deep, radial = held.shape
    thetas = rows - 4
    axials = deep - 2 * PAD

    for c in range(comps):
        held[c, i + 2, PAD - 2 : PAD, :] = lo_ref[c, i]
        held[c, i + 2, PAD + axials : PAD + axials + 2, :] = hi_ref[c, i]

    size = min(axials, 32)
    shape = (size, radial)
    lane = iota(shape, 1)
    radius, inv_arc = radial_constants(radial, spacing, shape)
    outward = (radius + 1.0) / radius
    inward = (radius - 1.0) / radius
    signs = (1.0, -1.0, -1.0, 1.0)

    for k in range(0, axials, size):
        flow = flows[i, k : k + size, :]
        scale = (0.5 * GAIN) / (flow + 2.0 + inv_arc)
        at = PAD + k

        def here(c, t, shift=0):
            return held[c, i + 2 + t, at + shift : at + shift + size, :]

        smooth, ahead, tilt = [], [], []
        for c in range(comps):
            now = here(c, 0)
            a1p, a1m = here(c, 0, 1), here(c, 0, -1)
            t1p, t1m = here(c, 1), here(c, -1)
            ghost = pole_ghost(pole_ref, c, k, size, i, thetas)
            if signs[c] < 0:
                ghost = -ghost
            inner = pltpu.roll(now, 1, 1)
            inner = jnp.concatenate(
                [jnp.where(lane[:, :LANES] == 0, ghost, inner[:, :LANES]), inner[:, LANES:]], axis=1
            )
            outer = jnp.where(lane == radial - 1, 0.0, pltpu.roll(now, radial - 1, 1))
            far = here(c, 2) + here(c, -2) + here(c, 0, 2) + here(c, 0, -2)
            near = t1p + t1m + a1p + a1m
            total = work[c, i, k : k + size, :] + RAD * (inner + outer)
            total = total + 4.0 * FOUR * near - FOUR * far - (2.0 * RAD + 12.0 * FOUR) * now
            smooth.append(total)
            ahead.append(a1p - a1m)
            if c == 0:
                p_theta = (t1p - t1m) * inv_arc
                p_radial = outer - inner
            elif c == 1:
                spread = outer * outward - inner * inward
            elif c == 2:
                t_theta = (t1p - t1m) * inv_arc
        gains = (
            spread + t_theta + ahead[3],
            p_radial,
            p_theta,
            ahead[0],
        )
        for c in range(comps):
            work[c, i, k : k + size, :] = smooth[c] - scale * (flow * ahead[c] + gains[c])


def section(state, base, flow, before, after, below, above, pole, spacing):
    comps, thetas, axials, radial = state.shape
    return pl.pallas_call(
        functools.partial(section_kernel, spacing),
        in_specs=[HBM, HBM, HBM, ANY, ANY, VMEM, VMEM, VMEM],
        out_specs=HBM,
        out_shape=jax.ShapeDtypeStruct(state.shape, state.dtype),
        scratch_shapes=[
            pltpu.VMEM((comps, thetas + 4, axials + 2 * PAD, radial), jnp.float32),
            pltpu.VMEM(state.shape, jnp.float32),
            pltpu.VMEM(flow.shape, jnp.float32),
            pltpu.SemaphoreType.DMA((5, thetas)),
        ],
        compiler_params=params(56),
        cost_estimate=cost(40 * state.size, 4 * (3 * state.size + flow.size)),
        name="section",
    )(state, base, flow, before, after, below, above, pole)


def patch(out, lines, rows, place):
    comps, thetas, axials, radial = out.shape
    parts = radial // LANES
    count = rows.shape[0]
    tiles = thetas * axials // 8
    wide = out.reshape(comps, tiles, 8, parts, LANES).transpose(0, 1, 3, 2, 4)
    wide = wide.reshape(comps, tiles, parts, 8, 1, LANES)
    lines = lines.reshape(lines.shape[0], comps, parts, 1, LANES)

    def kernel(rows_ref, place_ref, lines_ref, _, o_ref, sem):
        def copy(n):
            row = rows_ref[n]
            return pltpu.make_async_copy(
                lines_ref.at[place_ref[n]], o_ref.at[:, lax.shift_right_logical(row, 3), :, row & 7], sem
            )

        def start(n, _):
            copy(n).start()
            return 0

        lax.fori_loop(0, count, start, 0, unroll=8)
        pltpu.make_async_copy(
            lines_ref.at[pl.ds(0, count)], lines_ref.at[pl.ds(0, count)], sem
        ).wait()

    wide = pl.pallas_call(
        kernel,
        in_specs=[SMEM, SMEM, ANY, HBM],
        out_specs=HBM,
        out_shape=jax.ShapeDtypeStruct(wide.shape, wide.dtype),
        input_output_aliases={3: 0},
        scratch_shapes=[pltpu.SemaphoreType.DMA],
        compiler_params=params(4),
        cost_estimate=cost(0, 2 * count * comps * radial * 4),
        name="patch",
    )(rows, place, lines, wide)
    wide = wide.reshape(comps, tiles, parts, 8, LANES).transpose(0, 1, 3, 2, 4)
    return wide.reshape(out.shape)


def behind(value, done):
    return lax.optimization_barrier((value, done))


def per_device(state, base, flow, fin, receptor_rows, donor_owner, donor_local, weights):
    comps, thetas, axials, radial = state.shape
    n_az, n_ax = lax.axis_size("az"), lax.axis_size("ax")
    devices = n_az * n_ax
    receptors = receptor_rows.shape[0]
    cap = max(2, 2 * receptors // devices)
    halves = 2 if n_ax % 2 == 0 else 1
    half = n_ax // halves
    spacing = 2.0 * math.pi / (thetas * n_az)
    both = ("az", "ax")
    groups = [
        [a * n_ax + h * half + q for a in range(n_az) for q in range(half)] for h in range(halves)
    ]
    my_half = (lax.axis_index("ax") // half).reshape(1).astype(jnp.int32)

    def exchange(x):
        return lax.all_to_all(x, both, 0, 0, axis_index_groups=groups, tiled=True)

    def around(x, by):
        return lax.ppermute(x, "az", [(a, (a + by) % n_az) for a in range(n_az)])

    def along(x, by):
        return lax.ppermute(x, "ax", [(a, a + by) for a in range(n_ax) if 0 <= a + by < n_ax])

    blocks = [fin]
    if halves == 2:
        blocks.append(lax.ppermute(fin, "ax", [(a, (a + half) % n_ax) for a in range(n_ax)]))
    first, last = theta_edges(state)
    before, after = around(last, 1), around(first, -1)
    owner, first = behind(donor_owner[:, 0], first)
    table, place = requests(
        owner, donor_local, weights, n_az, n_ax, halves, my_half, cap, fin.shape[0]
    )
    asked = exchange(table)
    later, table = behind(state, table)
    low, high, pole = inner_edges(later)
    below, above = along(high, 1), along(low, -1)
    asked, low, before = lax.optimization_barrier((asked, low, before))
    pole = around(pole, n_az // 2)
    lines = interpolate(
        asked[:, 0], [lines_of(b) for b in blocks], halves * cap, comps, radial
    )
    lines, before, after, below, above, pole = lax.optimization_barrier(
        (lines, before, after, below, above, pole)
    )
    base, lines = behind(base, lines)
    lines = exchange(lines)
    out = section(state, base, flow, before, after, below, above, pole, spacing)
    return patch(out, lines, receptor_rows, place.reshape(receptors))


def solution(mesh):
    placed = (
        P(None, "az", "ax", None),
        P(None, "az", "ax", None),
        P("az", "ax", None),
        P(("az", "ax"), None, None),
        P(("az", "ax")),
        P(("az", "ax"), None),
        P(("az", "ax")),
        P(("az", "ax"), None),
    )
    return jax.shard_map(
        per_device, mesh=mesh, in_specs=placed, out_specs=P(None, "az", "ax", None), check_vma=False
    )
```

```python
import functools
import math

import jax
import jax.numpy as jnp
from jax import lax
from jax.experimental import pallas as pl
from jax.experimental.pallas import tpu as pltpu
from jax.sharding import PartitionSpec as P

COURANT = 1.2
SECOND = 0.25
FOURTH = 0.03125
SECTION_WEIGHT = 0.6

GAIN = SECTION_WEIGHT * COURANT
FOUR = GAIN * FOURTH
RAD = GAIN * SECOND
LANES = 128
PAD = 8
GROUP = 2
AHEAD = 5
TALL = 20
ANY = pl.BlockSpec(memory_space=pl.ANY)
HBM = pl.BlockSpec(memory_space=pltpu.HBM)
VMEM = pl.BlockSpec(memory_space=pltpu.VMEM)
SMEM = pl.BlockSpec(memory_space=pltpu.SMEM)


def params(mib):
    return pltpu.CompilerParams(vmem_limit_bytes=mib * 2**20)


def cost(flops, moved):
    return pl.CostEstimate(flops=flops // 1000, bytes_accessed=moved // 1000, transcendentals=0)


def iota(shape, dim):
    return lax.broadcasted_iota(jnp.int32, shape, dim)


def theta_edges(state):
    comps, thetas, axials, radial = state.shape

    def kernel(s_ref, first_ref, last_ref, held, sems):
        def copies(n):
            side, c = n % 2, n // 2
            at, out = ((0, first_ref), (thetas - 2, last_ref))[side]
            return (
                pltpu.make_async_copy(s_ref.at[c, pl.ds(at, 2)], held.at[n], sems.at[0, n]),
                pltpu.make_async_copy(held.at[n], out.at[c], sems.at[1, n]),
            )

        moves = [copies(n) for n in range(2 * comps)]
        for come, _ in moves:
            come.start()
        for come, go in moves:
            come.wait()
            go.start()
        for _, go in moves:
            go.wait()

    edge = jax.ShapeDtypeStruct((comps, 2, axials, radial), state.dtype)
    return pl.pallas_call(
        kernel,
        in_specs=[HBM],
        out_specs=(HBM, HBM),
        out_shape=(edge, edge),
        scratch_shapes=[
            pltpu.VMEM((2 * comps, 2, axials, radial), jnp.float32),
            pltpu.SemaphoreType.DMA((2, 2 * comps)),
        ],
        compiler_params=params(60),
        cost_estimate=cost(0, 4 * edge.size * 4),
        name="theta_edges",
    )(state)


def pole_fold(thetas, axials):
    fold = LANES // thetas if LANES % thetas == 0 else 1
    while fold > 1 and axials % (8 * fold):
        fold //= 2
    return fold


def inner_edges(state):
    comps, thetas, axials, radial = state.shape
    fold = pole_fold(thetas, axials)
    part = axials // fold
    width = max(LANES, -(-thetas // LANES) * LANES)
    group = 4

    def kernel(s_ref, first_ref, last_ref, pole_ref, core, low, high, sems):
        def core_copy(t):
            return pltpu.make_async_copy(
                s_ref.at[:, t, :, pl.ds(0, LANES)], core.at[:, t], sems.at[0, t]
            )

        def edge_copy(g, at, out, n):
            rows = pl.ds(g * group, group)
            return pltpu.make_async_copy(
                s_ref.at[:, rows, pl.ds(at, 8), :], out.at[:, rows], sems.at[n, g]
            )

        for t in range(thetas):
            core_copy(t).start()
            if t % group == 0:
                edge_copy(t // group, 0, low, 1).start()
                edge_copy(t // group, axials - 8, high, 2).start()
        lane = iota((part, width), 1)
        pole_ref[...] = jnp.zeros_like(pole_ref)

        def body(g, _):
            for u in range(group):
                core_copy(g * group + u).wait()
            edge_copy(g, 0, low, 1).wait()
            edge_copy(g, axials - 8, high, 2).wait()
            for u in range(group):
                i = g * group + u
                for c in range(comps):
                    first_ref[c, i] = low[c, i, 0:2, :]
                    last_ref[c, i] = high[c, i, 6:8, :]
            for c in range(comps):
                packed = pole_ref[c]
                for u in range(group):
                    i = g * group + u
                    for f in range(fold):
                        column = core[c, i, f * part : (f + 1) * part, 0:1]
                        column = jnp.broadcast_to(column, (part, width))
                        packed = jnp.where(lane == i + f * thetas, column, packed)
                pole_ref[c] = packed
            return 0

        lax.fori_loop(0, thetas // group, body, 0)

    edge = jax.ShapeDtypeStruct((comps, thetas, 2, radial), state.dtype)
    pole = jax.ShapeDtypeStruct((comps, part, width), state.dtype)
    return pl.pallas_call(
        kernel,
        in_specs=[HBM],
        out_specs=(VMEM, VMEM, VMEM),
        out_shape=(edge, edge, pole),
        scratch_shapes=[
            pltpu.VMEM((comps, thetas, axials, LANES), jnp.float32),
            pltpu.VMEM((comps, thetas, 8, radial), jnp.float32),
            pltpu.VMEM((comps, thetas, 8, radial), jnp.float32),
            pltpu.SemaphoreType.DMA((3, thetas)),
        ],
        compiler_params=params(60),
        cost_estimate=cost(state.size, 6 * 2**20),
        name="inner_edges",
    )(state)


def requests(owner, local, weights, n_az, n_ax, halves, my_half, cap, rows_dev):
    receptors = local.shape[0]
    half = n_ax // halves
    holders = n_az * half
    slots = halves * cap
    total = holders * slots
    width = -(-3 * slots // LANES) * LANES
    wide = max(total, width)

    def kernel(half_ref, owner_ref, local_ref, w_ref, table_ref, place_ref):
        square = (receptors, receptors)
        own_row = jnp.broadcast_to(owner_ref[...], square)
        down, across = iota(square, 0), iota(square, 1)
        same = down == across
        zero = jnp.zeros(square, jnp.int32)
        own_col = jnp.sum(jnp.where(same, own_row, zero), axis=1, keepdims=True)
        alike = own_row == own_col
        one = jnp.ones(square, jnp.int32)

        def place(own, rank):
            az, ax = own // n_ax, own % n_ax
            away = jnp.where(ax // half == half_ref[0], 0, 1) if halves > 1 else 0 * ax
            return (az * half + ax % half) * slots + away * cap + rank, away

        rank_row = jnp.sum(jnp.where(alike & (down < across), one, zero), axis=0, keepdims=True)
        rank_col = jnp.sum(jnp.where(alike & (across < down), one, zero), axis=1, keepdims=True)
        place_ref[...] = place(owner_ref[...], rank_row)[0]
        spot, away = place(own_col, rank_col)
        loc_row = jnp.broadcast_to(local_ref[...], square)
        line = jnp.sum(jnp.where(same, loc_row, zero), axis=1, keepdims=True) + away * rows_dev
        hit = iota((receptors, wide), 1) == spot
        fields = []
        for value in (line.astype(jnp.float32), w_ref[:, 0:1], w_ref[:, 1:2]):
            fields.append(jnp.sum(jnp.where(hit, value, 0.0), axis=0, keepdims=True))
        lane = iota((1, width), 1)
        for g in range(holders):
            packed = jnp.zeros((1, width), jnp.float32)
            for f, field in enumerate(fields):
                moved = pltpu.roll(field, (f * slots - g * slots) % wide, 1)[:, :width]
                packed = jnp.where(lane // slots == f, moved, packed)
            table_ref[g] = jnp.broadcast_to(packed, (TALL, width))

    return pl.pallas_call(
        kernel,
        in_specs=[SMEM, VMEM, VMEM, VMEM],
        out_specs=(VMEM, VMEM),
        out_shape=(
            jax.ShapeDtypeStruct((holders, TALL, width), jnp.float32),
            jax.ShapeDtypeStruct((1, receptors), jnp.int32),
        ),
        compiler_params=params(8),
        cost_estimate=cost(receptors * wide * 8, 2**17),
        name="requests",
    )(my_half, owner.reshape(1, receptors), local.reshape(1, receptors), weights)


def lines_of(fin):
    rows, comps, radial = fin.shape
    parts = radial // LANES
    return fin.reshape(rows, comps, parts, LANES).transpose(0, 2, 1, 3).reshape(rows * parts * comps, LANES)


def interpolate(table, blocks, slots, comps, radial):
    holders = table.shape[0]
    parts = radial // LANES
    line = comps * parts
    rows = blocks[0].shape[0]
    count = len(blocks)

    def kernel(*refs):
        t_ref, block_refs, out_ref, held = refs[0], refs[1 : 1 + count], refs[1 + count], refs[2 + count]
        per = rows // line
        for b, ref in enumerate(block_refs):
            for c in range(comps):
                for q in range(parts):
                    taken = ref[pl.ds(q * comps + c, per, stride=line), :]
                    held[pl.ds(b * rows + c * parts + q, per, stride=line), :] = taken

        def body(g, _):
            for s in range(slots):
                at = t_ref[g, s].astype(jnp.int32) * line
                at = pl.multiple_of(at, line)
                lower = held[pl.ds(at, line), :]
                upper = held[pl.ds(pl.multiple_of(at + line, line), line), :]
                out_ref[g * slots + s] = t_ref[g, slots + s] * lower + t_ref[g, 2 * slots + s] * upper
            return 0

        lax.fori_loop(0, holders, body, 0)

    return pl.pallas_call(
        kernel,
        in_specs=[SMEM] + [VMEM] * count,
        out_specs=VMEM,
        out_shape=jax.ShapeDtypeStruct((holders * slots, line, LANES), jnp.float32),
        scratch_shapes=[pltpu.VMEM((rows * count + line, LANES), jnp.float32)],
        compiler_params=params(8),
        cost_estimate=cost(holders * slots * line * LANES * 3, 2 * 2**20),
        name="interpolate",
    )(table, *blocks)


def radial_constants(radial, spacing, shape):
    j = iota(shape, len(shape) - 1).astype(jnp.float32)
    radius = j + 0.5
    inv_arc = 1.0 / (radius * spacing)
    return radius, inv_arc


def section_kernel(spacing, *refs):
    s_hbm, b_hbm, w_hbm, before, after, lo_ref, hi_ref, pole_ref, o_hbm, held, work, flows, mixed, mix, sems = refs
    comps, rows, deep, radial = held.shape
    thetas = rows - 4
    axials = deep - 2 * PAD
    groups = thetas // GROUP
    inside = pl.ds(PAD, axials)

    def copy_in(g, which):
        some = pl.ds(g * GROUP, GROUP)
        if which == 0:
            source, target = s_hbm.at[:, some], held.at[:, pl.ds(g * GROUP + 2, GROUP), inside, :]
        elif which == 1:
            source, target = b_hbm.at[:, some], work.at[:, some]
        else:
            source, target = w_hbm.at[some], flows.at[some]
        return pltpu.make_async_copy(source, target, sems.at[which, g])

    def store(g):
        some = pl.ds(g * GROUP, GROUP)
        return pltpu.make_async_copy(work.at[:, some], o_hbm.at[:, some], sems.at[3, g])

    def halo(side):
        source, at = ((before, 0), (after, rows - 2))[side]
        return pltpu.make_async_copy(source, held.at[:, pl.ds(at, 2), inside, :], sems.at[4, side])

    def begin(g):
        for which in range(3):
            copy_in(g, which).start()

    halo(0).start()
    for g in range(min(AHEAD, groups)):
        begin(g)
    halo(1).start()
    halo(0).wait()
    copy_in(0, 0).wait()

    one = axial_mix(axials)
    mix[...] = jnp.concatenate([one, one, one], axis=1).astype(jnp.bfloat16)

    def step(g, _):
        @pl.when(g + AHEAD < groups)
        def _():
            begin(g + AHEAD)

        @pl.when(g + 1 < groups)
        def _():
            copy_in(g + 1, 0).wait()

        @pl.when(g + 1 == groups)
        def _():
            halo(1).wait()

        copy_in(g, 1).wait()
        copy_in(g, 2).wait()
        for u in range(GROUP):
            section_row(g * GROUP + u, spacing, lo_ref, hi_ref, pole_ref, mix, held, work, flows, mixed)
        store(g).start()
        return 0

    lax.fori_loop(0, groups, step, 0)

    def drain(g, _):
        store(g).wait()
        return 0

    lax.fori_loop(0, groups, drain, 0)


def neighbours(now, sign, ghost):
    size, radial = now.shape
    lane = iota((size, LANES), 1)
    parts = [now[:, at : at + LANES] for at in range(0, radial, LANES)]
    up = [pltpu.roll(x, 1, 1) for x in parts]
    down = [pltpu.roll(x, LANES - 1, 1) for x in parts]
    inner = [jnp.where(lane == 0, low, x) for low, x in zip([ghost if sign > 0 else -ghost] + up, up)]
    zero = jnp.zeros_like(ghost)
    outer = [jnp.where(lane == LANES - 1, high, x) for high, x in zip(down[1:] + [zero], down)]
    return jnp.concatenate(inner, axis=1), jnp.concatenate(outer, axis=1)


def pole_ghost(pole_ref, c, k, size, i, thetas):
    part, width = pole_ref.shape[1:]
    pieces = []
    while size > 0:
        f, at = k // part, k % part
        take = min(size, part - at)
        piece = pole_ref[c, at : at + take, :]
        pieces.append(pltpu.roll(piece, width - i - f * thetas, 1)[:, :LANES])
        k, size = k + take, size - take
    return jnp.concatenate(pieces, axis=0) if len(pieces) > 1 else pieces[0]


def section_row(i, spacing, lo_ref, hi_ref, pole_ref, mix, held, work, flows, mixed):
    comps, rows, deep, radial = held.shape
    thetas = rows - 4
    axials = deep - 2 * PAD

    blank = jnp.zeros((PAD - 2, radial), jnp.float32)
    for c in range(comps):
        column = jnp.concatenate(
            [blank, lo_ref[c, i], held[c, i + 2, PAD : PAD + axials, :], hi_ref[c, i], blank], axis=0
        )
        high = column.astype(jnp.bfloat16)
        rest = column - high.astype(jnp.float32)
        middle = rest.astype(jnp.bfloat16)
        low = (rest - middle.astype(jnp.float32)).astype(jnp.bfloat16)
        split = jnp.concatenate([high, middle, low], axis=0)
        mixed[c] = jnp.dot(mix[...], split, preferred_element_type=jnp.float32)

    size = 16
    shape = (size, radial)
    radius, inv_arc = radial_constants(radial, spacing, shape)
    outward = (radius + 1.0) / radius
    inward = (radius - 1.0) / radius
    signs = (1.0, -1.0, -1.0, 1.0)

    for k in range(0, axials, size):
        flow = flows[i, k : k + size, :]
        scale = (0.5 * GAIN) / (flow + 2.0 + inv_arc)
        at = PAD + k

        def here(c, t):
            return held[c, i + 2 + t, at : at + size, :]

        def turned(c):
            now = here(c, 0)
            t1p, t1m = here(c, 1), here(c, -1)
            inner, outer = neighbours(now, signs[c], pole_ghost(pole_ref, c, k, size, i, thetas))
            far = here(c, 2) + here(c, -2)
            total = work[c, i, k : k + size, :] + RAD * (inner + outer)
            total = total + 4.0 * FOUR * (t1p + t1m) - FOUR * (far - mixed[c, k : k + size, :])
            total = total - (2.0 * RAD + 12.0 * FOUR) * now
            return total, mixed[c, axials + k : axials + k + size, :], inner, outer, t1p, t1m

        def put(c, total, ahead, gain):
            work[c, i, k : k + size, :] = total - scale * (flow * ahead + gain)

        total0, ahead0, inner, outer, t1p, t1m = turned(0)
        p_radial, p_theta = outer - inner, (t1p - t1m) * inv_arc
        total, ahead, inner, outer, _, _ = turned(1)
        gain0 = outer * outward - inner * inward
        put(1, total, ahead, p_radial)
        total, ahead, _, _, t1p, t1m = turned(2)
        gain0 = gain0 + (t1p - t1m) * inv_arc
        put(2, total, ahead, p_theta)
        total, ahead, _, _, _, _ = turned(3)
        put(3, total, ahead, ahead0)
        put(0, total0, ahead0, gain0 + ahead)


def axial_mix(axials):
    shape = (axials, axials + 2 * PAD)
    off = iota(shape, 1) - PAD - iota(shape, 0)
    near, far = jnp.abs(off) == 1, jnp.abs(off) == 2
    smooth = jnp.where(near, 4.0, jnp.where(far, -1.0, 0.0))
    slope = jnp.where(near, off.astype(jnp.float32), 0.0)
    return jnp.concatenate([smooth, slope], axis=0)


def section(state, base, flow, before, after, below, above, pole, spacing):
    comps, thetas, axials, radial = state.shape
    return pl.pallas_call(
        functools.partial(section_kernel, spacing),
        in_specs=[HBM, HBM, HBM, ANY, ANY, VMEM, VMEM, VMEM],
        out_specs=HBM,
        out_shape=jax.ShapeDtypeStruct(state.shape, state.dtype),
        scratch_shapes=[
            pltpu.VMEM((comps, thetas + 4, axials + 2 * PAD, radial), jnp.float32),
            pltpu.VMEM(state.shape, jnp.float32),
            pltpu.VMEM(flow.shape, jnp.float32),
            pltpu.VMEM((comps, 2 * axials, radial), jnp.float32),
            pltpu.VMEM((2 * axials, 3 * (axials + 2 * PAD)), jnp.bfloat16),
            pltpu.SemaphoreType.DMA((5, thetas)),
        ],
        compiler_params=params(56),
        cost_estimate=cost(40 * state.size, 4 * (3 * state.size + flow.size)),
        name="section",
    )(state, base, flow, before, after, below, above, pole)


def patch(out, lines, rows, place):
    comps, thetas, axials, radial = out.shape
    parts = radial // LANES
    count = rows.shape[0]
    tiles = thetas * axials // 8
    wide = out.reshape(comps, tiles, 8, parts, LANES).transpose(0, 1, 3, 2, 4)
    wide = wide.reshape(comps, tiles, parts, 8, 1, LANES)
    lines = lines.reshape(lines.shape[0], comps, parts, 1, LANES)

    def kernel(rows_ref, place_ref, lines_ref, _, o_ref, sem):
        def copy(n):
            row = rows_ref[n]
            return pltpu.make_async_copy(
                lines_ref.at[place_ref[n]], o_ref.at[:, lax.shift_right_logical(row, 3), :, row & 7], sem
            )

        def start(n, _):
            copy(n).start()
            return 0

        lax.fori_loop(0, count, start, 0, unroll=8)
        pltpu.make_async_copy(
            lines_ref.at[pl.ds(0, count)], lines_ref.at[pl.ds(0, count)], sem
        ).wait()

    wide = pl.pallas_call(
        kernel,
        in_specs=[SMEM, SMEM, ANY, HBM],
        out_specs=HBM,
        out_shape=jax.ShapeDtypeStruct(wide.shape, wide.dtype),
        input_output_aliases={3: 0},
        scratch_shapes=[pltpu.SemaphoreType.DMA],
        compiler_params=params(4),
        cost_estimate=cost(0, 2 * count * comps * radial * 4),
        name="patch",
    )(rows, place, lines, wide)
    wide = wide.reshape(comps, tiles, parts, 8, LANES).transpose(0, 1, 3, 2, 4)
    return wide.reshape(out.shape)


def behind(value, done):
    return lax.optimization_barrier((value, done))


def per_device(state, base, flow, fin, receptor_rows, donor_owner, donor_local, weights):
    comps, thetas, axials, radial = state.shape
    n_az, n_ax = lax.axis_size("az"), lax.axis_size("ax")
    devices = n_az * n_ax
    receptors = receptor_rows.shape[0]
    cap = max(2, 2 * receptors // devices)
    halves = 2 if n_ax % 2 == 0 else 1
    half = n_ax // halves
    spacing = 2.0 * math.pi / (thetas * n_az)
    both = ("az", "ax")
    groups = [
        [a * n_ax + h * half + q for a in range(n_az) for q in range(half)] for h in range(halves)
    ]
    my_half = (lax.axis_index("ax") // half).reshape(1).astype(jnp.int32)

    def exchange(x):
        return lax.all_to_all(x, both, 0, 0, axis_index_groups=groups, tiled=True)

    def around(x, by):
        return lax.ppermute(x, "az", [(a, (a + by) % n_az) for a in range(n_az)])

    def along(x, by):
        return lax.ppermute(x, "ax", [(a, a + by) for a in range(n_ax) if 0 <= a + by < n_ax])

    blocks = [fin]
    if halves == 2:
        blocks.append(lax.ppermute(fin, "ax", [(a, (a + half) % n_ax) for a in range(n_ax)]))
    first, last = theta_edges(state)
    before, after = around(last, 1), around(first, -1)
    owner, first = behind(donor_owner[:, 0], first)
    table, place = requests(
        owner, donor_local, weights, n_az, n_ax, halves, my_half, cap, fin.shape[0]
    )
    asked = exchange(table)
    later, table = behind(state, table)
    low, high, pole = inner_edges(later)
    below, above = along(high, 1), along(low, -1)
    asked, low, before = lax.optimization_barrier((asked, low, before))
    pole = around(pole, n_az // 2)
    lines = interpolate(
        asked[:, 0], [lines_of(b) for b in blocks], halves * cap, comps, radial
    )
    lines, before, after, below, above, pole = lax.optimization_barrier(
        (lines, before, after, below, above, pole)
    )
    base, lines = behind(base, lines)
    lines = exchange(lines)
    out = section(state, base, flow, before, after, below, above, pole, spacing)
    return patch(out, lines, receptor_rows, place.reshape(receptors))


def solution(mesh):
    placed = (
        P(None, "az", "ax", None),
        P(None, "az", "ax", None),
        P("az", "ax", None),
        P(("az", "ax"), None, None),
        P(("az", "ax")),
        P(("az", "ax"), None),
        P(("az", "ax")),
        P(("az", "ax"), None),
    )
    return jax.shard_map(
        per_device, mesh=mesh, in_specs=placed, out_specs=P(None, "az", "ax", None), check_vma=False
    )
```

```python
import functools
import math

import jax
import jax.numpy as jnp
from jax import lax
from jax.experimental import pallas as pl
from jax.experimental.pallas import tpu as pltpu
from jax.sharding import PartitionSpec as P

COURANT = 1.2
SECOND = 0.25
FOURTH = 0.03125
SECTION_WEIGHT = 0.6

GAIN = SECTION_WEIGHT * COURANT
FOUR = GAIN * FOURTH
RAD = GAIN * SECOND
LANES = 128
PAD = 8
GROUP = 2
AHEAD = 5

ANY = pl.BlockSpec(memory_space=pl.ANY)
HBM = pl.BlockSpec(memory_space=pltpu.HBM)
VMEM = pl.BlockSpec(memory_space=pltpu.VMEM)
SMEM = pl.BlockSpec(memory_space=pltpu.SMEM)

def params(mib):
    return pltpu.CompilerParams(vmem_limit_bytes=mib * 2**20)

def cost(flops, moved):
    return pl.CostEstimate(flops=flops // 1000, bytes_accessed=moved // 1000, transcendentals=0)

def iota(shape, dim):
    return lax.broadcasted_iota(jnp.int32, shape, dim)


def theta_edges(state):
    comps, thetas, axials, radial = state.shape

    def kernel(s_ref, first_ref, last_ref, held, sems):
        def copies(n):
            side, c = n % 2, n // 2
            at, out = ((0, first_ref), (thetas - 2, last_ref))[side]
            return (
                pltpu.make_async_copy(s_ref.at[c, pl.ds(at, 2)], held.at[n], sems.at[0, n]),
                pltpu.make_async_copy(held.at[n], out.at[c], sems.at[1, n]),
            )

        moves = [copies(n) for n in range(2 * comps)]
        for come, _ in moves:
            come.start()
        for come, go in moves:
            come.wait()
            go.start()
        for _, go in moves:
            go.wait()

    edge = jax.ShapeDtypeStruct((comps, 2, axials, radial), state.dtype)
    return pl.pallas_call(
        kernel,
        in_specs=[HBM],
        out_specs=(HBM, HBM),
        out_shape=(edge, edge),
        scratch_shapes=[
            pltpu.VMEM((2 * comps, 2, axials, radial), jnp.float32),
            pltpu.SemaphoreType.DMA((2, 2 * comps)),
        ],
        compiler_params=params(60),
        cost_estimate=cost(0, 4 * edge.size * 4),
        name="theta_edges",
    )(state)


def pole_fold(thetas, axials):
    fold = LANES // thetas if LANES % thetas == 0 else 1
    while fold > 1 and axials % (8 * fold):
        fold //= 2
    return fold

def inner_edges(state):
    comps, thetas, axials, radial = state.shape
    fold = pole_fold(thetas, axials)
    part = axials // fold
    width = max(LANES, -(-thetas // LANES) * LANES)
    group = 4

    def kernel(s_ref, first_ref, last_ref, pole_ref, core, low, high, sems):
        def core_copy(t):
            return pltpu.make_async_copy(
                s_ref.at[:, t, :, pl.ds(0, LANES)], core.at[:, t], sems.at[0, t]
            )

        def edge_copy(g, at, out, n):
            rows = pl.ds(g * group, group)
            return pltpu.make_async_copy(
                s_ref.at[:, rows, pl.ds(at, 8), :], out.at[:, rows], sems.at[n, g]
            )

        for t in range(thetas):
            core_copy(t).start()
            if t % group == 0:
                edge_copy(t // group, 0, low, 1).start()
                edge_copy(t // group, axials - 8, high, 2).start()
        lane = iota((part, width), 1)
        pole_ref[...] = jnp.zeros_like(pole_ref)

        def body(g, _):
            for u in range(group):
                core_copy(g * group + u).wait()
            edge_copy(g, 0, low, 1).wait()
            edge_copy(g, axials - 8, high, 2).wait()
            for u in range(group):
                i = g * group + u
                for c in range(comps):
                    first_ref[c, i] = low[c, i, 0:2, :]
                    last_ref[c, i] = high[c, i, 6:8, :]
            for c in range(comps):
                packed = pole_ref[c]
                for u in range(group):
                    i = g * group + u
                    for f in range(fold):
                        column = core[c, i, f * part : (f + 1) * part, 0:1]
                        column = jnp.broadcast_to(column, (part, width))
                        packed = jnp.where(lane == i + f * thetas, column, packed)
                pole_ref[c] = packed
            return 0

        lax.fori_loop(0, thetas // group, body, 0)

    edge = jax.ShapeDtypeStruct((comps, thetas, 2, radial), state.dtype)
    pole = jax.ShapeDtypeStruct((comps, part, width), state.dtype)
    return pl.pallas_call(
        kernel,
        in_specs=[HBM],
        out_specs=(VMEM, VMEM, VMEM),
        out_shape=(edge, edge, pole),
        scratch_shapes=[
            pltpu.VMEM((comps, thetas, axials, LANES), jnp.float32),
            pltpu.VMEM((comps, thetas, 8, radial), jnp.float32),
            pltpu.VMEM((comps, thetas, 8, radial), jnp.float32),
            pltpu.SemaphoreType.DMA((3, thetas)),
        ],
        compiler_params=params(60),
        cost_estimate=cost(state.size, 6 * 2**20),
        name="inner_edges",
    )(state)


def requests(owner, local, weights, n_az, n_ax, halves, my_half, cap, rows_dev):
    receptors = local.shape[0]
    half = n_ax // halves
    holders = n_az * half
    slots = halves * cap
    total = holders * slots
    width = -(-3 * slots // LANES) * LANES
    wide = max(total, width)

    def kernel(half_ref, owner_ref, local_ref, w_ref, table_ref, place_ref):
        square = (receptors, receptors)
        own_row = jnp.broadcast_to(owner_ref[...], square)
        down, across = iota(square, 0), iota(square, 1)
        same = down == across
        zero = jnp.zeros(square, jnp.int32)
        own_col = jnp.sum(jnp.where(same, own_row, zero), axis=1, keepdims=True)
        alike = own_row == own_col
        one = jnp.ones(square, jnp.int32)

        def place(own, rank):
            az, ax = own // n_ax, own % n_ax
            away = jnp.where(ax // half == half_ref[0], 0, 1) if halves > 1 else 0 * ax
            return (az * half + ax % half) * slots + away * cap + rank, away

        rank_row = jnp.sum(jnp.where(alike & (down < across), one, zero), axis=0, keepdims=True)
        rank_col = jnp.sum(jnp.where(alike & (across < down), one, zero), axis=1, keepdims=True)
        place_ref[...] = place(owner_ref[...], rank_row)[0]
        spot, away = place(own_col, rank_col)
        loc_row = jnp.broadcast_to(local_ref[...], square)
        line = jnp.sum(jnp.where(same, loc_row, zero), axis=1, keepdims=True) + away * rows_dev
        hit = iota((receptors, wide), 1) == spot
        fields = []
        for value in (line.astype(jnp.float32), w_ref[:, 0:1], w_ref[:, 1:2]):
            fields.append(jnp.sum(jnp.where(hit, value, 0.0), axis=0, keepdims=True))
        lane = iota((1, width), 1)
        for g in range(holders):
            packed = jnp.zeros((1, width), jnp.float32)
            for f, field in enumerate(fields):
                moved = pltpu.roll(field, (f * slots - g * slots) % wide, 1)[:, :width]
                packed = jnp.where(lane // slots == f, moved, packed)
            table_ref[g] = packed

    return pl.pallas_call(
        kernel,
        in_specs=[SMEM, VMEM, VMEM, VMEM],
        out_specs=(VMEM, VMEM),
        out_shape=(
            jax.ShapeDtypeStruct((holders, 1, width), jnp.float32),
            jax.ShapeDtypeStruct((1, receptors), jnp.int32),
        ),
        compiler_params=params(8),
        cost_estimate=cost(receptors * wide * 8, 2**17),
        name="requests",
    )(my_half, owner.reshape(1, receptors), local.reshape(1, receptors), weights)


def lines_of(fin):
    rows, comps, radial = fin.shape
    parts = radial // LANES
    return fin.reshape(rows, comps, parts, LANES).transpose(0, 2, 1, 3).reshape(rows * parts * comps, LANES)

def interpolate(table, blocks, slots, comps, radial):
    holders = table.shape[0]
    parts = radial // LANES
    line = comps * parts
    rows = blocks[0].shape[0]
    count = len(blocks)

    def kernel(*refs):
        t_ref, block_refs, out_ref, held = refs[0], refs[1 : 1 + count], refs[1 + count], refs[2 + count]
        per = rows // line
        for b, ref in enumerate(block_refs):
            for c in range(comps):
                for q in range(parts):
                    taken = ref[pl.ds(q * comps + c, per, stride=line), :]
                    held[pl.ds(b * rows + c * parts + q, per, stride=line), :] = taken

        def body(g, _):
            for s in range(slots):
                at = t_ref[g, s].astype(jnp.int32) * line
                at = pl.multiple_of(at, line)
                lower = held[pl.ds(at, line), :]
                upper = held[pl.ds(pl.multiple_of(at + line, line), line), :]
                out_ref[g * slots + s] = t_ref[g, slots + s] * lower + t_ref[g, 2 * slots + s] * upper
            return 0

        lax.fori_loop(0, holders, body, 0)

    return pl.pallas_call(
        kernel,
        in_specs=[SMEM] + [VMEM] * count,
        out_specs=VMEM,
        out_shape=jax.ShapeDtypeStruct((holders * slots, line, LANES), jnp.float32),
        scratch_shapes=[pltpu.VMEM((rows * count + line, LANES), jnp.float32)],
        compiler_params=params(8),
        cost_estimate=pl.CostEstimate(flops=10**10, bytes_accessed=2**21, transcendentals=0),
        name="interpolate",
    )(table, *blocks)


def radial_constants(radial, spacing, shape):
    j = iota(shape, len(shape) - 1).astype(jnp.float32)
    radius = j + 0.5
    inv_arc = 1.0 / (radius * spacing)
    return radius, inv_arc

def section_kernel(spacing, *refs):
    s_hbm, b_hbm, w_hbm, before, after, lo_ref, hi_ref, pole_ref, o_hbm, held, work, flows, mixed, mix, sems = refs
    comps, rows, deep, radial = held.shape
    thetas = rows - 4
    axials = deep - 2 * PAD
    groups = thetas // GROUP
    inside = pl.ds(PAD, axials)

    def copy_in(g, which):
        some = pl.ds(g * GROUP, GROUP)
        if which == 0:
            source, target = s_hbm.at[:, some], held.at[:, pl.ds(g * GROUP + 2, GROUP), inside, :]
        elif which == 1:
            source, target = b_hbm.at[:, some], work.at[:, some]
        else:
            source, target = w_hbm.at[some], flows.at[some]
        return pltpu.make_async_copy(source, target, sems.at[which, g])

    def store(g):
        some = pl.ds(g * GROUP, GROUP)
        return pltpu.make_async_copy(work.at[:, some], o_hbm.at[:, some], sems.at[3, g])

    def halo(side):
        source, at = ((before, 0), (after, rows - 2))[side]
        return pltpu.make_async_copy(source, held.at[:, pl.ds(at, 2), inside, :], sems.at[4, side])

    def begin(g):
        for which in range(3):
            copy_in(g, which).start()

    halo(0).start()
    for g in range(min(AHEAD, groups)):
        begin(g)
    halo(1).start()
    halo(0).wait()
    copy_in(0, 0).wait()

    one = axial_mix(axials)
    mix[...] = jnp.concatenate([one, one, one], axis=1).astype(jnp.bfloat16)

    def step(g, _):
        @pl.when(g + AHEAD < groups)
        def _():
            begin(g + AHEAD)

        @pl.when(g + 1 < groups)
        def _():
            copy_in(g + 1, 0).wait()

        @pl.when(g + 1 == groups)
        def _():
            halo(1).wait()

        copy_in(g, 1).wait()
        copy_in(g, 2).wait()
        for u in range(GROUP):
            section_row(g * GROUP + u, spacing, lo_ref, hi_ref, pole_ref, mix, held, work, flows, mixed)
        store(g).start()
        return 0

    lax.fori_loop(0, groups, step, 0)

    def drain(g, _):
        store(g).wait()
        return 0

    lax.fori_loop(0, groups, drain, 0)

def neighbours(now, sign, ghost):
    size, radial = now.shape
    lane = iota((size, LANES), 1)
    parts = [now[:, at : at + LANES] for at in range(0, radial, LANES)]
    up = [pltpu.roll(x, 1, 1) for x in parts]
    down = [pltpu.roll(x, LANES - 1, 1) for x in parts]
    inner = [jnp.where(lane == 0, low, x) for low, x in zip([ghost if sign > 0 else -ghost] + up, up)]
    zero = jnp.zeros_like(ghost)
    outer = [jnp.where(lane == LANES - 1, high, x) for high, x in zip(down[1:] + [zero], down)]
    return jnp.concatenate(inner, axis=1), jnp.concatenate(outer, axis=1)

def pole_ghost(pole_ref, c, k, size, i, thetas):
    part, width = pole_ref.shape[1:]
    pieces = []
    while size > 0:
        f, at = k // part, k % part
        take = min(size, part - at)
        piece = pole_ref[c, at : at + take, :]
        pieces.append(pltpu.roll(piece, width - i - f * thetas, 1)[:, :LANES])
        k, size = k + take, size - take
    return jnp.concatenate(pieces, axis=0) if len(pieces) > 1 else pieces[0]

def section_row(i, spacing, lo_ref, hi_ref, pole_ref, mix, held, work, flows, mixed):
    comps, rows, deep, radial = held.shape
    thetas = rows - 4
    axials = deep - 2 * PAD

    blank = jnp.zeros((PAD - 2, radial), jnp.float32)
    for c in range(comps):
        column = jnp.concatenate(
            [blank, lo_ref[c, i], held[c, i + 2, PAD : PAD + axials, :], hi_ref[c, i], blank], axis=0
        )
        high = column.astype(jnp.bfloat16)
        rest = column - high.astype(jnp.float32)
        middle = rest.astype(jnp.bfloat16)
        low = (rest - middle.astype(jnp.float32)).astype(jnp.bfloat16)
        split = jnp.concatenate([high, middle, low], axis=0)
        mixed[c] = jnp.dot(mix[...], split, preferred_element_type=jnp.float32)

    size = 16
    shape = (size, radial)
    radius, inv_arc = radial_constants(radial, spacing, shape)
    outward = (radius + 1.0) / radius
    inward = (radius - 1.0) / radius
    signs = (1.0, -1.0, -1.0, 1.0)

    for k in range(0, axials, size):
        flow = flows[i, k : k + size, :]
        scale = (0.5 * GAIN) / (flow + 2.0 + inv_arc)
        at = PAD + k

        def here(c, t):
            return held[c, i + 2 + t, at : at + size, :]

        def turned(c):
            now = here(c, 0)
            t1p, t1m = here(c, 1), here(c, -1)
            inner, outer = neighbours(now, signs[c], pole_ghost(pole_ref, c, k, size, i, thetas))
            far = here(c, 2) + here(c, -2)
            total = work[c, i, k : k + size, :] + RAD * (inner + outer)
            total = total + 4.0 * FOUR * (t1p + t1m) - FOUR * (far - mixed[c, k : k + size, :])
            total = total - (2.0 * RAD + 12.0 * FOUR) * now
            return total, mixed[c, axials + k : axials + k + size, :], inner, outer, t1p, t1m

        def put(c, total, ahead, gain):
            work[c, i, k : k + size, :] = total - scale * (flow * ahead + gain)

        total0, ahead0, inner, outer, t1p, t1m = turned(0)
        p_radial, p_theta = outer - inner, (t1p - t1m) * inv_arc
        total, ahead, inner, outer, _, _ = turned(1)
        gain0 = outer * outward - inner * inward
        put(1, total, ahead, p_radial)
        total, ahead, _, _, t1p, t1m = turned(2)
        gain0 = gain0 + (t1p - t1m) * inv_arc
        put(2, total, ahead, p_theta)
        total, ahead, _, _, _, _ = turned(3)
        put(3, total, ahead, ahead0)
        put(0, total0, ahead0, gain0 + ahead)

def axial_mix(axials):
    shape = (axials, axials + 2 * PAD)
    off = iota(shape, 1) - PAD - iota(shape, 0)
    near, far = jnp.abs(off) == 1, jnp.abs(off) == 2
    smooth = jnp.where(near, 4.0, jnp.where(far, -1.0, 0.0))
    slope = jnp.where(near, off.astype(jnp.float32), 0.0)
    return jnp.concatenate([smooth, slope], axis=0)

def section(state, base, flow, before, after, below, above, pole, spacing):
    comps, thetas, axials, radial = state.shape
    return pl.pallas_call(
        functools.partial(section_kernel, spacing),
        in_specs=[HBM, HBM, HBM, ANY, ANY, VMEM, VMEM, VMEM],
        out_specs=HBM,
        out_shape=jax.ShapeDtypeStruct(state.shape, state.dtype),
        scratch_shapes=[
            pltpu.VMEM((comps, thetas + 4, axials + 2 * PAD, radial), jnp.float32),
            pltpu.VMEM(state.shape, jnp.float32),
            pltpu.VMEM(flow.shape, jnp.float32),
            pltpu.VMEM((comps, 2 * axials, radial), jnp.float32),
            pltpu.VMEM((2 * axials, 3 * (axials + 2 * PAD)), jnp.bfloat16),
            pltpu.SemaphoreType.DMA((5, thetas)),
        ],
        compiler_params=params(56),
        cost_estimate=cost(40 * state.size, 4 * (3 * state.size + flow.size)),
        name="section",
    )(state, base, flow, before, after, below, above, pole)


def patch(out, lines, rows, place):
    comps, thetas, axials, radial = out.shape
    parts = radial // LANES
    count = rows.shape[0]
    tiles = thetas * axials // 8
    wide = out.reshape(comps, tiles, 8, parts, LANES).transpose(0, 1, 3, 2, 4)
    wide = wide.reshape(comps, tiles, parts, 8, 1, LANES)
    lines = lines.reshape(lines.shape[0], comps, parts, 1, LANES)

    def kernel(rows_ref, place_ref, lines_ref, _, o_ref, sem):
        def copy(n):
            row = rows_ref[n]
            return pltpu.make_async_copy(
                lines_ref.at[place_ref[n]], o_ref.at[:, lax.shift_right_logical(row, 3), :, row & 7], sem
            )

        def start(n, _):
            copy(n).start()
            return 0

        lax.fori_loop(0, count, start, 0, unroll=8)
        pltpu.make_async_copy(
            lines_ref.at[pl.ds(0, count)], lines_ref.at[pl.ds(0, count)], sem
        ).wait()

    wide = pl.pallas_call(
        kernel,
        in_specs=[SMEM, SMEM, ANY, HBM],
        out_specs=HBM,
        out_shape=jax.ShapeDtypeStruct(wide.shape, wide.dtype),
        input_output_aliases={3: 0},
        scratch_shapes=[pltpu.SemaphoreType.DMA],
        compiler_params=params(4),
        cost_estimate=cost(0, 2 * count * comps * radial * 4),
        name="patch",
    )(rows, place, lines, wide)
    wide = wide.reshape(comps, tiles, parts, 8, LANES).transpose(0, 1, 3, 2, 4)
    return wide.reshape(out.shape)

def behind(value, done):
    return lax.optimization_barrier((value, done))

def per_device(state, base, flow, fin, receptor_rows, donor_owner, donor_local, weights):
    comps, thetas, axials, radial = state.shape
    n_az, n_ax = lax.axis_size("az"), lax.axis_size("ax")
    devices = n_az * n_ax
    receptors = receptor_rows.shape[0]
    cap = max(2, 2 * receptors // devices)
    halves = 2 if n_ax % 2 == 0 else 1
    half = n_ax // halves
    spacing = 2.0 * math.pi / (thetas * n_az)
    both = ("az", "ax")
    groups = [
        [a * n_ax + h * half + q for a in range(n_az) for q in range(half)] for h in range(halves)
    ]
    my_half = (lax.axis_index("ax") // half).reshape(1).astype(jnp.int32)

    def exchange(x):
        return lax.all_to_all(x, both, 0, 0, axis_index_groups=groups, tiled=True)

    def around(x, by):
        return lax.ppermute(x, "az", [(a, (a + by) % n_az) for a in range(n_az)])

    def along(x, by):
        return lax.ppermute(x, "ax", [(a, a + by) for a in range(n_ax) if 0 <= a + by < n_ax])

    blocks = [fin]
    if halves == 2:
        blocks.append(lax.ppermute(fin, "ax", [(a, (a + half) % n_ax) for a in range(n_ax)]))
    first, last = theta_edges(state)
    before, after = around(last, 1), around(first, -1)
    owner, first = behind(donor_owner[:, 0], first)
    table, place = requests(
        owner, donor_local, weights, n_az, n_ax, halves, my_half, cap, fin.shape[0]
    )
    asked = exchange(table)
    later, table = behind(state, table)
    low, high, pole = inner_edges(later)
    below, above = along(high, 1), along(low, -1)
    asked, low, before = lax.optimization_barrier((asked, low, before))
    pole = around(pole, n_az // 2)
    lines = interpolate(
        asked[:, 0], [lines_of(b) for b in blocks], halves * cap, comps, radial
    )
    lines, before, after, below, above, pole = lax.optimization_barrier(
        (lines, before, after, below, above, pole)
    )
    base, lines = behind(base, lines)
    lines = exchange(lines)
    out = section(state, base, flow, before, after, below, above, pole, spacing)
    return patch(out, lines, receptor_rows, place.reshape(receptors))

def solution(mesh):
    placed = (
        P(None, "az", "ax", None),
        P(None, "az", "ax", None),
        P("az", "ax", None),
        P(("az", "ax"), None, None),
        P(("az", "ax")),
        P(("az", "ax"), None),
        P(("az", "ax")),
        P(("az", "ax"), None),
    )
    return jax.shard_map(
        per_device, mesh=mesh, in_specs=placed, out_specs=P(None, "az", "ax", None), check_vma=False
    )
```

```python
import functools
import math

import jax
import jax.numpy as jnp
from jax import lax
from jax.experimental import pallas as pl
from jax.experimental.pallas import tpu as pltpu
from jax.sharding import PartitionSpec as P

COURANT = 1.2
SECOND = 0.25
FOURTH = 0.03125
SECTION_WEIGHT = 0.6

GAIN = SECTION_WEIGHT * COURANT
FOUR = GAIN * FOURTH
RAD = GAIN * SECOND
LANES = 128
PAD = 8
GROUP = 2
AHEAD = 5

ANY = pl.BlockSpec(memory_space=pl.ANY)
HBM = pl.BlockSpec(memory_space=pltpu.HBM)
VMEM = pl.BlockSpec(memory_space=pltpu.VMEM)
SMEM = pl.BlockSpec(memory_space=pltpu.SMEM)

def params(mib):
    return pltpu.CompilerParams(vmem_limit_bytes=mib * 2**20)

def cost(flops, moved):
    return pl.CostEstimate(flops=flops // 1000, bytes_accessed=moved // 1000, transcendentals=0)

def iota(shape, dim):
    return lax.broadcasted_iota(jnp.int32, shape, dim)


def theta_edges(state):
    comps, thetas, axials, radial = state.shape

    def kernel(s_ref, first_ref, last_ref, held, sems):
        def copies(n):
            side, c = n % 2, n // 2
            at, out = ((0, first_ref), (thetas - 2, last_ref))[side]
            return (
                pltpu.make_async_copy(s_ref.at[c, pl.ds(at, 2)], held.at[n], sems.at[0, n]),
                pltpu.make_async_copy(held.at[n], out.at[c], sems.at[1, n]),
            )

        moves = [copies(n) for n in range(2 * comps)]
        for come, _ in moves:
            come.start()
        for come, go in moves:
            come.wait()
            go.start()
        for _, go in moves:
            go.wait()

    edge = jax.ShapeDtypeStruct((comps, 2, axials, radial), state.dtype)
    return pl.pallas_call(
        kernel,
        in_specs=[HBM],
        out_specs=(HBM, HBM),
        out_shape=(edge, edge),
        scratch_shapes=[
            pltpu.VMEM((2 * comps, 2, axials, radial), jnp.float32),
            pltpu.SemaphoreType.DMA((2, 2 * comps)),
        ],
        compiler_params=params(60),
        cost_estimate=cost(0, 4 * edge.size * 4),
        name="theta_edges",
    )(state)


def pole_fold(thetas, axials):
    fold = LANES // thetas if LANES % thetas == 0 else 1
    while fold > 1 and axials % (8 * fold):
        fold //= 2
    return fold

def inner_edges(state):
    comps, thetas, axials, radial = state.shape
    fold = pole_fold(thetas, axials)
    part = axials // fold
    width = max(LANES, -(-thetas // LANES) * LANES)
    group = 4

    def kernel(s_ref, first_ref, last_ref, pole_ref, core, sems):
        def core_copy(t):
            return pltpu.make_async_copy(s_ref.at[:, t], core.at[:, t], sems.at[t])

        for t in range(thetas):
            core_copy(t).start()
        lane = iota((part, width), 1)
        pole_ref[...] = jnp.zeros_like(pole_ref)

        def body(g, _):
            for u in range(group):
                core_copy(g * group + u).wait()
            for u in range(group):
                i = g * group + u
                for c in range(comps):
                    first_ref[c, i] = core[c, i, 0:2, :]
                    last_ref[c, i] = core[c, i, axials - 2 : axials, :]
            for c in range(comps):
                packed = pole_ref[c]
                for u in range(group):
                    i = g * group + u
                    for f in range(fold):
                        column = core[c, i, f * part : (f + 1) * part, 0:LANES][:, 0:1]
                        column = jnp.broadcast_to(column, (part, width))
                        packed = jnp.where(lane == i + f * thetas, column, packed)
                pole_ref[c] = packed
            return 0

        lax.fori_loop(0, thetas // group, body, 0)

    edge = jax.ShapeDtypeStruct((comps, thetas, 2, radial), state.dtype)
    pole = jax.ShapeDtypeStruct((comps, part, width), state.dtype)
    return pl.pallas_call(
        kernel,
        in_specs=[HBM],
        out_specs=(VMEM, VMEM, VMEM),
        out_shape=(edge, edge, pole),
        scratch_shapes=[
            pltpu.VMEM(state.shape, jnp.float32),
            pltpu.SemaphoreType.DMA((thetas,)),
        ],
        compiler_params=params(60),
        cost_estimate=cost(state.size, 6 * 2**20),
        name="inner_edges",
    )(state)


def requests(owner, local, weights, n_az, n_ax, halves, my_half, cap, rows_dev):
    receptors = local.shape[0]
    half = n_ax // halves
    holders = n_az * half
    slots = halves * cap
    total = holders * slots
    width = -(-3 * slots // LANES) * LANES
    wide = max(total, width)

    def kernel(half_ref, owner_ref, local_ref, w_ref, table_ref, place_ref):
        square = (receptors, receptors)
        own_row = jnp.broadcast_to(owner_ref[...], square)
        down, across = iota(square, 0), iota(square, 1)
        same = down == across
        zero = jnp.zeros(square, jnp.int32)
        own_col = jnp.sum(jnp.where(same, own_row, zero), axis=1, keepdims=True)
        alike = own_row == own_col
        one = jnp.ones(square, jnp.int32)

        def place(own, rank):
            az, ax = own // n_ax, own % n_ax
            away = jnp.where(ax // half == half_ref[0], 0, 1) if halves > 1 else 0 * ax
            return (az * half + ax % half) * slots + away * cap + rank, away

        rank_row = jnp.sum(jnp.where(alike & (down < across), one, zero), axis=0, keepdims=True)
        rank_col = jnp.sum(jnp.where(alike & (across < down), one, zero), axis=1, keepdims=True)
        place_ref[...] = place(owner_ref[...], rank_row)[0]
        spot, away = place(own_col, rank_col)
        loc_row = jnp.broadcast_to(local_ref[...], square)
        line = jnp.sum(jnp.where(same, loc_row, zero), axis=1, keepdims=True) + away * rows_dev
        hit = iota((receptors, wide), 1) == spot
        fields = []
        for value in (line.astype(jnp.float32), w_ref[:, 0:1], w_ref[:, 1:2]):
            fields.append(jnp.sum(jnp.where(hit, value, 0.0), axis=0, keepdims=True))
        lane = iota((1, width), 1)
        for g in range(holders):
            packed = jnp.zeros((1, width), jnp.float32)
            for f, field in enumerate(fields):
                moved = pltpu.roll(field, (f * slots - g * slots) % wide, 1)[:, :width]
                packed = jnp.where(lane // slots == f, moved, packed)
            table_ref[g] = packed

    return pl.pallas_call(
        kernel,
        in_specs=[SMEM, VMEM, VMEM, VMEM],
        out_specs=(VMEM, VMEM),
        out_shape=(
            jax.ShapeDtypeStruct((holders, 1, width), jnp.float32),
            jax.ShapeDtypeStruct((1, receptors), jnp.int32),
        ),
        compiler_params=params(8),
        cost_estimate=cost(receptors * wide * 8, 2**17),
        name="requests",
    )(my_half, owner.reshape(1, receptors), local.reshape(1, receptors), weights)


def lines_of(fin):
    rows, comps, radial = fin.shape
    parts = radial // LANES
    return fin.reshape(rows, comps, parts, LANES).transpose(0, 2, 1, 3).reshape(rows * parts * comps, LANES)

def interpolate(table, blocks, slots, comps, radial):
    holders = table.shape[0]
    parts = radial // LANES
    line = comps * parts
    rows = blocks[0].shape[0]
    count = len(blocks)

    def kernel(*refs):
        t_ref, block_refs, out_ref, held = refs[0], refs[1 : 1 + count], refs[1 + count], refs[2 + count]
        per = rows // line
        for b, ref in enumerate(block_refs):
            for c in range(comps):
                for q in range(parts):
                    taken = ref[pl.ds(q * comps + c, per, stride=line), :]
                    held[pl.ds(b * rows + c * parts + q, per, stride=line), :] = taken

        def body(g, _):
            for s in range(slots):
                at = t_ref[g, s].astype(jnp.int32) * line
                at = pl.multiple_of(at, line)
                lower = held[pl.ds(at, line), :]
                upper = held[pl.ds(pl.multiple_of(at + line, line), line), :]
                out_ref[g * slots + s] = t_ref[g, slots + s] * lower + t_ref[g, 2 * slots + s] * upper
            return 0

        lax.fori_loop(0, holders, body, 0)

    return pl.pallas_call(
        kernel,
        in_specs=[SMEM] + [VMEM] * count,
        out_specs=VMEM,
        out_shape=jax.ShapeDtypeStruct((holders * slots, line, LANES), jnp.float32),
        scratch_shapes=[pltpu.VMEM((rows * count + line, LANES), jnp.float32)],
        compiler_params=params(8),
        cost_estimate=pl.CostEstimate(flops=10**10, bytes_accessed=2**21, transcendentals=0),
        name="interpolate",
    )(table, *blocks)


def radial_constants(radial, spacing, shape):
    j = iota(shape, len(shape) - 1).astype(jnp.float32)
    radius = j + 0.5
    inv_arc = 1.0 / (radius * spacing)
    return radius, inv_arc

def section_kernel(spacing, *refs):
    s_hbm, b_hbm, w_hbm, before, after, lo_ref, hi_ref, pole_ref, o_hbm, held, work, flows, mixed, mix, sems = refs
    comps, rows, deep, radial = held.shape
    thetas = rows - 4
    axials = deep - 2 * PAD
    groups = thetas // GROUP
    inside = pl.ds(PAD, axials)

    def copy_in(g, which):
        some = pl.ds(g * GROUP, GROUP)
        if which == 0:
            source, target = s_hbm.at[:, some], held.at[:, pl.ds(g * GROUP + 2, GROUP), inside, :]
        elif which == 1:
            source, target = b_hbm.at[:, some], work.at[:, some]
        else:
            source, target = w_hbm.at[some], flows.at[some]
        return pltpu.make_async_copy(source, target, sems.at[which, g])

    def store(g):
        some = pl.ds(g * GROUP, GROUP)
        return pltpu.make_async_copy(work.at[:, some], o_hbm.at[:, some], sems.at[3, g])

    def halo(side):
        source, at = ((before, 0), (after, rows - 2))[side]
        return pltpu.make_async_copy(source, held.at[:, pl.ds(at, 2), inside, :], sems.at[4, side])

    def begin(g):
        for which in range(3):
            copy_in(g, which).start()

    halo(0).start()
    for g in range(min(AHEAD, groups)):
        begin(g)
    halo(1).start()
    halo(0).wait()
    copy_in(0, 0).wait()

    one = axial_mix(axials)
    mix[...] = jnp.concatenate([one, one, one], axis=1).astype(jnp.bfloat16)

    def step(g, _):
        @pl.when(g + AHEAD < groups)
        def _():
            begin(g + AHEAD)

        @pl.when(g + 1 < groups)
        def _():
            copy_in(g + 1, 0).wait()

        @pl.when(g + 1 == groups)
        def _():
            halo(1).wait()

        copy_in(g, 1).wait()
        copy_in(g, 2).wait()
        for u in range(GROUP):
            section_row(g * GROUP + u, spacing, lo_ref, hi_ref, pole_ref, mix, held, work, flows, mixed)
        store(g).start()
        return 0

    lax.fori_loop(0, groups, step, 0)

    def drain(g, _):
        store(g).wait()
        return 0

    lax.fori_loop(0, groups, drain, 0)

def neighbours(now, sign, ghost):
    size, radial = now.shape
    lane = iota((size, LANES), 1)
    parts = [now[:, at : at + LANES] for at in range(0, radial, LANES)]
    up = [pltpu.roll(x, 1, 1) for x in parts]
    down = [pltpu.roll(x, LANES - 1, 1) for x in parts]
    inner = [jnp.where(lane == 0, low, x) for low, x in zip([ghost if sign > 0 else -ghost] + up, up)]
    zero = jnp.zeros_like(ghost)
    outer = [jnp.where(lane == LANES - 1, high, x) for high, x in zip(down[1:] + [zero], down)]
    return jnp.concatenate(inner, axis=1), jnp.concatenate(outer, axis=1)

def pole_ghost(pole_ref, c, k, size, i, thetas):
    part, width = pole_ref.shape[1:]
    pieces = []
    while size > 0:
        f, at = k // part, k % part
        take = min(size, part - at)
        piece = pole_ref[c, at : at + take, :]
        pieces.append(pltpu.roll(piece, width - i - f * thetas, 1)[:, :LANES])
        k, size = k + take, size - take
    return jnp.concatenate(pieces, axis=0) if len(pieces) > 1 else pieces[0]

def section_row(i, spacing, lo_ref, hi_ref, pole_ref, mix, held, work, flows, mixed):
    comps, rows, deep, radial = held.shape
    thetas = rows - 4
    axials = deep - 2 * PAD

    blank = jnp.zeros((PAD - 2, radial), jnp.float32)
    for c in range(comps):
        column = jnp.concatenate(
            [blank, lo_ref[c, i], held[c, i + 2, PAD : PAD + axials, :], hi_ref[c, i], blank], axis=0
        )
        high = column.astype(jnp.bfloat16)
        rest = column - high.astype(jnp.float32)
        middle = rest.astype(jnp.bfloat16)
        low = (rest - middle.astype(jnp.float32)).astype(jnp.bfloat16)
        split = jnp.concatenate([high, middle, low], axis=0)
        mixed[c] = jnp.dot(mix[...], split, preferred_element_type=jnp.float32)

    size = 16
    shape = (size, radial)
    radius, inv_arc = radial_constants(radial, spacing, shape)
    outward = (radius + 1.0) / radius
    inward = (radius - 1.0) / radius
    signs = (1.0, -1.0, -1.0, 1.0)

    for k in range(0, axials, size):
        flow = flows[i, k : k + size, :]
        scale = (0.5 * GAIN) / (flow + 2.0 + inv_arc)
        at = PAD + k

        def here(c, t):
            return held[c, i + 2 + t, at : at + size, :]

        def turned(c):
            now = here(c, 0)
            t1p, t1m = here(c, 1), here(c, -1)
            inner, outer = neighbours(now, signs[c], pole_ghost(pole_ref, c, k, size, i, thetas))
            far = here(c, 2) + here(c, -2)
            total = work[c, i, k : k + size, :] + RAD * (inner + outer)
            total = total + 4.0 * FOUR * (t1p + t1m) - FOUR * (far - mixed[c, k : k + size, :])
            total = total - (2.0 * RAD + 12.0 * FOUR) * now
            return total, mixed[c, axials + k : axials + k + size, :], inner, outer, t1p, t1m

        def put(c, total, ahead, gain):
            work[c, i, k : k + size, :] = total - scale * (flow * ahead + gain)

        total0, ahead0, inner, outer, t1p, t1m = turned(0)
        p_radial, p_theta = outer - inner, (t1p - t1m) * inv_arc
        total, ahead, inner, outer, _, _ = turned(1)
        gain0 = outer * outward - inner * inward
        put(1, total, ahead, p_radial)
        total, ahead, _, _, t1p, t1m = turned(2)
        gain0 = gain0 + (t1p - t1m) * inv_arc
        put(2, total, ahead, p_theta)
        total, ahead, _, _, _, _ = turned(3)
        put(3, total, ahead, ahead0)
        put(0, total0, ahead0, gain0 + ahead)

def axial_mix(axials):
    shape = (axials, axials + 2 * PAD)
    off = iota(shape, 1) - PAD - iota(shape, 0)
    near, far = jnp.abs(off) == 1, jnp.abs(off) == 2
    smooth = jnp.where(near, 4.0, jnp.where(far, -1.0, 0.0))
    slope = jnp.where(near, off.astype(jnp.float32), 0.0)
    return jnp.concatenate([smooth, slope], axis=0)

def section(state, base, flow, before, after, below, above, pole, spacing):
    comps, thetas, axials, radial = state.shape
    return pl.pallas_call(
        functools.partial(section_kernel, spacing),
        in_specs=[HBM, HBM, HBM, ANY, ANY, VMEM, VMEM, VMEM],
        out_specs=HBM,
        out_shape=jax.ShapeDtypeStruct(state.shape, state.dtype),
        scratch_shapes=[
            pltpu.VMEM((comps, thetas + 4, axials + 2 * PAD, radial), jnp.float32),
            pltpu.VMEM(state.shape, jnp.float32),
            pltpu.VMEM(flow.shape, jnp.float32),
            pltpu.VMEM((comps, 2 * axials, radial), jnp.float32),
            pltpu.VMEM((2 * axials, 3 * (axials + 2 * PAD)), jnp.bfloat16),
            pltpu.SemaphoreType.DMA((5, thetas)),
        ],
        compiler_params=params(56),
        cost_estimate=cost(40 * state.size, 4 * (3 * state.size + flow.size)),
        name="section",
    )(state, base, flow, before, after, below, above, pole)


def patch(out, lines, rows, place):
    comps, thetas, axials, radial = out.shape
    parts = radial // LANES
    count = rows.shape[0]
    tiles = thetas * axials // 8
    wide = out.reshape(comps, tiles, 8, parts, LANES).transpose(0, 1, 3, 2, 4)
    wide = wide.reshape(comps, tiles, parts, 8, 1, LANES)
    lines = lines.reshape(lines.shape[0], comps, parts, 1, LANES)

    def kernel(rows_ref, place_ref, lines_ref, _, o_ref, sem):
        def copy(n):
            row = rows_ref[n]
            return pltpu.make_async_copy(
                lines_ref.at[place_ref[n]], o_ref.at[:, lax.shift_right_logical(row, 3), :, row & 7], sem
            )

        def start(n, _):
            copy(n).start()
            return 0

        lax.fori_loop(0, count, start, 0, unroll=8)
        pltpu.make_async_copy(
            lines_ref.at[pl.ds(0, count)], lines_ref.at[pl.ds(0, count)], sem
        ).wait()

    wide = pl.pallas_call(
        kernel,
        in_specs=[SMEM, SMEM, ANY, HBM],
        out_specs=HBM,
        out_shape=jax.ShapeDtypeStruct(wide.shape, wide.dtype),
        input_output_aliases={3: 0},
        scratch_shapes=[pltpu.SemaphoreType.DMA],
        compiler_params=params(4),
        cost_estimate=cost(0, 2 * count * comps * radial * 4),
        name="patch",
    )(rows, place, lines, wide)
    wide = wide.reshape(comps, tiles, parts, 8, LANES).transpose(0, 1, 3, 2, 4)
    return wide.reshape(out.shape)

def behind(value, done):
    return lax.optimization_barrier((value, done))

def per_device(state, base, flow, fin, receptor_rows, donor_owner, donor_local, weights):
    comps, thetas, axials, radial = state.shape
    n_az, n_ax = lax.axis_size("az"), lax.axis_size("ax")
    devices = n_az * n_ax
    receptors = receptor_rows.shape[0]
    cap = max(2, 2 * receptors // devices)
    halves = 2 if n_ax % 2 == 0 else 1
    half = n_ax // halves
    spacing = 2.0 * math.pi / (thetas * n_az)
    both = ("az", "ax")
    groups = [
        [a * n_ax + h * half + q for a in range(n_az) for q in range(half)] for h in range(halves)
    ]
    my_half = (lax.axis_index("ax") // half).reshape(1).astype(jnp.int32)

    def exchange(x):
        return lax.all_to_all(x, both, 0, 0, axis_index_groups=groups, tiled=True)

    def around(x, by):
        return lax.ppermute(x, "az", [(a, (a + by) % n_az) for a in range(n_az)])

    def along(x, by):
        return lax.ppermute(x, "ax", [(a, a + by) for a in range(n_ax) if 0 <= a + by < n_ax])

    blocks = [fin]
    if halves == 2:
        blocks.append(lax.ppermute(fin, "ax", [(a, (a + half) % n_ax) for a in range(n_ax)]))
    first, last = theta_edges(state)
    before, after = around(last, 1), around(first, -1)
    owner, first = behind(donor_owner[:, 0], first)
    table, place = requests(
        owner, donor_local, weights, n_az, n_ax, halves, my_half, cap, fin.shape[0]
    )
    asked = exchange(table)
    later, table = behind(state, table)
    low, high, pole = inner_edges(later)
    below, above = along(high, 1), along(low, -1)
    asked, low, before = lax.optimization_barrier((asked, low, before))
    pole = around(pole, n_az // 2)
    lines = interpolate(
        asked[:, 0], [lines_of(b) for b in blocks], halves * cap, comps, radial
    )
    lines, before, after, below, above, pole = lax.optimization_barrier(
        (lines, before, after, below, above, pole)
    )
    base, lines = behind(base, lines)
    lines = exchange(lines)
    out = section(state, base, flow, before, after, below, above, pole, spacing)
    return patch(out, lines, receptor_rows, place.reshape(receptors))

def solution(mesh):
    placed = (
        P(None, "az", "ax", None),
        P(None, "az", "ax", None),
        P("az", "ax", None),
        P(("az", "ax"), None, None),
        P(("az", "ax")),
        P(("az", "ax"), None),
        P(("az", "ax")),
        P(("az", "ax"), None),
    )
    return jax.shard_map(
        per_device, mesh=mesh, in_specs=placed, out_specs=P(None, "az", "ax", None), check_vma=False
    )
```

```python
import functools
import math

import jax
import jax.numpy as jnp
from jax import lax
from jax.experimental import pallas as pl
from jax.experimental.pallas import tpu as pltpu
from jax.sharding import PartitionSpec as P

COURANT = 1.2
SECOND = 0.25
FOURTH = 0.03125
SECTION_WEIGHT = 0.6

GAIN = SECTION_WEIGHT * COURANT
FOUR = GAIN * FOURTH
RAD = GAIN * SECOND
LANES = 128
PAD = 8
GROUP = 2
AHEAD = 5

ANY = pl.BlockSpec(memory_space=pl.ANY)
HBM = pl.BlockSpec(memory_space=pltpu.HBM)
VMEM = pl.BlockSpec(memory_space=pltpu.VMEM)
SMEM = pl.BlockSpec(memory_space=pltpu.SMEM)

def params(mib):
    return pltpu.CompilerParams(vmem_limit_bytes=mib * 2**20)

def cost(flops, moved):
    return pl.CostEstimate(flops=flops // 1000, bytes_accessed=moved // 1000, transcendentals=0)

def iota(shape, dim):
    return lax.broadcasted_iota(jnp.int32, shape, dim)


def theta_edges(state):
    comps, thetas, axials, radial = state.shape

    def kernel(s_ref, first_ref, last_ref, held, sems):
        def copies(n):
            side, c = n % 2, n // 2
            at, out = ((0, first_ref), (thetas - 2, last_ref))[side]
            return (
                pltpu.make_async_copy(s_ref.at[c, pl.ds(at, 2)], held.at[n], sems.at[0, n]),
                pltpu.make_async_copy(held.at[n], out.at[c], sems.at[1, n]),
            )

        moves = [copies(n) for n in range(2 * comps)]
        for come, _ in moves:
            come.start()
        for come, go in moves:
            come.wait()
            go.start()
        for _, go in moves:
            go.wait()

    edge = jax.ShapeDtypeStruct((comps, 2, axials, radial), state.dtype)
    return pl.pallas_call(
        kernel,
        in_specs=[HBM],
        out_specs=(HBM, HBM),
        out_shape=(edge, edge),
        scratch_shapes=[
            pltpu.VMEM((2 * comps, 2, axials, radial), jnp.float32),
            pltpu.SemaphoreType.DMA((2, 2 * comps)),
        ],
        compiler_params=params(60),
        cost_estimate=cost(0, 4 * edge.size * 4),
        name="theta_edges",
    )(state)


def pole_fold(thetas, axials):
    fold = LANES // thetas if LANES % thetas == 0 else 1
    while fold > 1 and axials % (8 * fold):
        fold //= 2
    return fold

def inner_edges(state):
    comps, thetas, axials, radial = state.shape
    fold = pole_fold(thetas, axials)
    part = axials // fold
    width = max(LANES, -(-thetas // LANES) * LANES)
    group = 8 if thetas % 8 == 0 else 4

    def kernel(s_ref, first_ref, last_ref, pole_ref, core, sems):
        def core_copy(t):
            return pltpu.make_async_copy(s_ref.at[:, t], core.at[:, t], sems.at[t])

        for t in range(thetas):
            core_copy(t).start()
        lane = iota((part, width), 1)
        pole_ref[...] = jnp.zeros_like(pole_ref)

        def body(g, _):
            for u in range(group):
                core_copy(g * group + u).wait()
            for u in range(group):
                i = g * group + u
                for c in range(comps):
                    first_ref[c, i] = core[c, i, 0:2, :]
                    last_ref[c, i] = core[c, i, axials - 2 : axials, :]
            for c in range(comps):
                packed = pole_ref[c]
                for u in range(group):
                    i = g * group + u
                    for f in range(fold):
                        column = core[c, i, f * part : (f + 1) * part, 0:LANES][:, 0:1]
                        column = jnp.broadcast_to(column, (part, width))
                        packed = jnp.where(lane == i + f * thetas, column, packed)
                pole_ref[c] = packed
            return 0

        lax.fori_loop(0, thetas // group, body, 0)

    edge = jax.ShapeDtypeStruct((comps, thetas, 2, radial), state.dtype)
    pole = jax.ShapeDtypeStruct((comps, part, width), state.dtype)
    return pl.pallas_call(
        kernel,
        in_specs=[HBM],
        out_specs=(VMEM, VMEM, VMEM),
        out_shape=(edge, edge, pole),
        scratch_shapes=[
            pltpu.VMEM(state.shape, jnp.float32),
            pltpu.SemaphoreType.DMA((thetas,)),
        ],
        compiler_params=params(60),
        cost_estimate=cost(state.size, 6 * 2**20),
        name="inner_edges",
    )(state)


def requests(owner, local, weights, n_az, n_ax, halves, my_half, cap, rows_dev):
    receptors = local.shape[0]
    half = n_ax // halves
    holders = n_az * half
    slots = halves * cap
    total = holders * slots
    width = -(-3 * slots // LANES) * LANES
    wide = max(total, width)

    def kernel(half_ref, owner_ref, local_ref, w_ref, table_ref, place_ref):
        square = (receptors, receptors)
        own_row = jnp.broadcast_to(owner_ref[...], square)
        down, across = iota(square, 0), iota(square, 1)
        same = down == across
        zero = jnp.zeros(square, jnp.int32)
        own_col = jnp.sum(jnp.where(same, own_row, zero), axis=1, keepdims=True)
        alike = own_row == own_col
        one = jnp.ones(square, jnp.int32)

        def place(own, rank):
            az, ax = own // n_ax, own % n_ax
            away = jnp.where(ax // half == half_ref[0], 0, 1) if halves > 1 else 0 * ax
            return (az * half + ax % half) * slots + away * cap + rank, away

        rank_row = jnp.sum(jnp.where(alike & (down < across), one, zero), axis=0, keepdims=True)
        rank_col = jnp.sum(jnp.where(alike & (across < down), one, zero), axis=1, keepdims=True)
        place_ref[...] = place(owner_ref[...], rank_row)[0]
        spot, away = place(own_col, rank_col)
        loc_row = jnp.broadcast_to(local_ref[...], square)
        line = jnp.sum(jnp.where(same, loc_row, zero), axis=1, keepdims=True) + away * rows_dev
        hit = iota((receptors, wide), 1) == spot
        fields = []
        for value in (line.astype(jnp.float32), w_ref[:, 0:1], w_ref[:, 1:2]):
            fields.append(jnp.sum(jnp.where(hit, value, 0.0), axis=0, keepdims=True))
        lane = iota((1, width), 1)
        for g in range(holders):
            packed = jnp.zeros((1, width), jnp.float32)
            for f, field in enumerate(fields):
                moved = pltpu.roll(field, (f * slots - g * slots) % wide, 1)[:, :width]
                packed = jnp.where(lane // slots == f, moved, packed)
            table_ref[g] = packed

    return pl.pallas_call(
        kernel,
        in_specs=[SMEM, VMEM, VMEM, VMEM],
        out_specs=(VMEM, VMEM),
        out_shape=(
            jax.ShapeDtypeStruct((holders, 1, width), jnp.float32),
            jax.ShapeDtypeStruct((1, receptors), jnp.int32),
        ),
        compiler_params=params(8),
        cost_estimate=cost(receptors * wide * 8, 2**17),
        name="requests",
    )(my_half, owner.reshape(1, receptors), local.reshape(1, receptors), weights)


def lines_of(fin):
    rows, comps, radial = fin.shape
    parts = radial // LANES
    return fin.reshape(rows, comps, parts, LANES).transpose(0, 2, 1, 3).reshape(rows * parts * comps, LANES)

def interpolate(table, blocks, slots, comps, radial):
    holders = table.shape[0]
    parts = radial // LANES
    line = comps * parts
    rows = blocks[0].shape[0]
    count = len(blocks)

    def kernel(*refs):
        t_ref, block_refs, out_ref, held = refs[0], refs[1 : 1 + count], refs[1 + count], refs[2 + count]
        per = rows // line
        for b, ref in enumerate(block_refs):
            for c in range(comps):
                for q in range(parts):
                    taken = ref[pl.ds(q * comps + c, per, stride=line), :]
                    held[pl.ds(b * rows + c * parts + q, per, stride=line), :] = taken

        def body(g, _):
            for s in range(slots):
                at = t_ref[g, s].astype(jnp.int32) * line
                at = pl.multiple_of(at, line)
                lower = held[pl.ds(at, line), :]
                upper = held[pl.ds(pl.multiple_of(at + line, line), line), :]
                out_ref[g * slots + s] = t_ref[g, slots + s] * lower + t_ref[g, 2 * slots + s] * upper
            return 0

        lax.fori_loop(0, holders, body, 0)

    return pl.pallas_call(
        kernel,
        in_specs=[SMEM] + [VMEM] * count,
        out_specs=VMEM,
        out_shape=jax.ShapeDtypeStruct((holders * slots, line, LANES), jnp.float32),
        scratch_shapes=[pltpu.VMEM((rows * count + line, LANES), jnp.float32)],
        compiler_params=params(8),
        cost_estimate=pl.CostEstimate(flops=10**10, bytes_accessed=2**21, transcendentals=0),
        name="interpolate",
    )(table, *blocks)


def radial_constants(radial, spacing, shape):
    j = iota(shape, len(shape) - 1).astype(jnp.float32)
    radius = j + 0.5
    inv_arc = 1.0 / (radius * spacing)
    return radius, inv_arc

def section_kernel(spacing, *refs):
    s_hbm, b_hbm, w_hbm, before, after, lo_ref, hi_ref, pole_ref, o_hbm, held, work, flows, mixed, mix, sems = refs
    comps, rows, deep, radial = held.shape
    thetas = rows - 4
    axials = deep - 2 * PAD
    groups = thetas // GROUP
    inside = pl.ds(PAD, axials)

    def copy_in(g, which):
        some = pl.ds(g * GROUP, GROUP)
        if which == 0:
            source, target = s_hbm.at[:, some], held.at[:, pl.ds(g * GROUP + 2, GROUP), inside, :]
        elif which == 1:
            source, target = b_hbm.at[:, some], work.at[:, some]
        else:
            source, target = w_hbm.at[some], flows.at[some]
        return pltpu.make_async_copy(source, target, sems.at[which, g])

    def store(g):
        some = pl.ds(g * GROUP, GROUP)
        return pltpu.make_async_copy(work.at[:, some], o_hbm.at[:, some], sems.at[3, g])

    def halo(side):
        source, at = ((before, 0), (after, rows - 2))[side]
        return pltpu.make_async_copy(source, held.at[:, pl.ds(at, 2), inside, :], sems.at[4, side])

    def begin(g):
        for which in range(3):
            copy_in(g, which).start()

    halo(0).start()
    for g in range(min(AHEAD, groups)):
        begin(g)
    halo(1).start()
    halo(0).wait()
    copy_in(0, 0).wait()

    one = axial_mix(axials)
    mix[...] = jnp.concatenate([one, one, one], axis=1).astype(jnp.bfloat16)

    def step(g, _):
        @pl.when(g + AHEAD < groups)
        def _():
            begin(g + AHEAD)

        @pl.when(g + 1 < groups)
        def _():
            copy_in(g + 1, 0).wait()

        @pl.when(g + 1 == groups)
        def _():
            halo(1).wait()

        copy_in(g, 1).wait()
        copy_in(g, 2).wait()
        for u in range(GROUP):
            section_row(g * GROUP + u, spacing, lo_ref, hi_ref, pole_ref, mix, held, work, flows, mixed)
        store(g).start()
        return 0

    lax.fori_loop(0, groups, step, 0)

    def drain(g, _):
        store(g).wait()
        return 0

    lax.fori_loop(0, groups, drain, 0)

def neighbours(now, sign, ghost):
    size, radial = now.shape
    lane = iota((size, LANES), 1)
    parts = [now[:, at : at + LANES] for at in range(0, radial, LANES)]
    up = [pltpu.roll(x, 1, 1) for x in parts]
    down = [pltpu.roll(x, LANES - 1, 1) for x in parts]
    inner = [jnp.where(lane == 0, low, x) for low, x in zip([ghost if sign > 0 else -ghost] + up, up)]
    zero = jnp.zeros_like(ghost)
    outer = [jnp.where(lane == LANES - 1, high, x) for high, x in zip(down[1:] + [zero], down)]
    return jnp.concatenate(inner, axis=1), jnp.concatenate(outer, axis=1)

def pole_ghost(pole_ref, c, k, size, i, thetas):
    part, width = pole_ref.shape[1:]
    pieces = []
    while size > 0:
        f, at = k // part, k % part
        take = min(size, part - at)
        piece = pole_ref[c, at : at + take, :]
        pieces.append(pltpu.roll(piece, width - i - f * thetas, 1)[:, :LANES])
        k, size = k + take, size - take
    return jnp.concatenate(pieces, axis=0) if len(pieces) > 1 else pieces[0]

def section_row(i, spacing, lo_ref, hi_ref, pole_ref, mix, held, work, flows, mixed):
    comps, rows, deep, radial = held.shape
    thetas = rows - 4
    axials = deep - 2 * PAD

    blank = jnp.zeros((PAD - 2, radial), jnp.float32)
    for c in range(comps):
        column = jnp.concatenate(
            [blank, lo_ref[c, i], held[c, i + 2, PAD : PAD + axials, :], hi_ref[c, i], blank], axis=0
        )
        high = column.astype(jnp.bfloat16)
        rest = column - high.astype(jnp.float32)
        middle = rest.astype(jnp.bfloat16)
        low = (rest - middle.astype(jnp.float32)).astype(jnp.bfloat16)
        split = jnp.concatenate([high, middle, low], axis=0)
        mixed[c] = jnp.dot(mix[...], split, preferred_element_type=jnp.float32)

    size = 16
    shape = (size, radial)
    radius, inv_arc = radial_constants(radial, spacing, shape)
    outward = (radius + 1.0) / radius
    inward = (radius - 1.0) / radius
    signs = (1.0, -1.0, -1.0, 1.0)

    for k in range(0, axials, size):
        flow = flows[i, k : k + size, :]
        scale = (0.5 * GAIN) / (flow + 2.0 + inv_arc)
        at = PAD + k

        def here(c, t):
            return held[c, i + 2 + t, at : at + size, :]

        def turned(c):
            now = here(c, 0)
            t1p, t1m = here(c, 1), here(c, -1)
            inner, outer = neighbours(now, signs[c], pole_ghost(pole_ref, c, k, size, i, thetas))
            far = here(c, 2) + here(c, -2)
            total = work[c, i, k : k + size, :] + RAD * (inner + outer)
            total = total + 4.0 * FOUR * (t1p + t1m) - FOUR * (far - mixed[c, k : k + size, :])
            total = total - (2.0 * RAD + 12.0 * FOUR) * now
            return total, mixed[c, axials + k : axials + k + size, :], inner, outer, t1p, t1m

        def put(c, total, ahead, gain):
            work[c, i, k : k + size, :] = total - scale * (flow * ahead + gain)

        total0, ahead0, inner, outer, t1p, t1m = turned(0)
        p_radial, p_theta = outer - inner, (t1p - t1m) * inv_arc
        total, ahead, inner, outer, _, _ = turned(1)
        gain0 = outer * outward - inner * inward
        put(1, total, ahead, p_radial)
        total, ahead, _, _, t1p, t1m = turned(2)
        gain0 = gain0 + (t1p - t1m) * inv_arc
        put(2, total, ahead, p_theta)
        total, ahead, _, _, _, _ = turned(3)
        put(3, total, ahead, ahead0)
        put(0, total0, ahead0, gain0 + ahead)

def axial_mix(axials):
    shape = (axials, axials + 2 * PAD)
    off = iota(shape, 1) - PAD - iota(shape, 0)
    near, far = jnp.abs(off) == 1, jnp.abs(off) == 2
    smooth = jnp.where(near, 4.0, jnp.where(far, -1.0, 0.0))
    slope = jnp.where(near, off.astype(jnp.float32), 0.0)
    return jnp.concatenate([smooth, slope], axis=0)

def section(state, base, flow, before, after, below, above, pole, spacing):
    comps, thetas, axials, radial = state.shape
    return pl.pallas_call(
        functools.partial(section_kernel, spacing),
        in_specs=[HBM, HBM, HBM, ANY, ANY, VMEM, VMEM, VMEM],
        out_specs=HBM,
        out_shape=jax.ShapeDtypeStruct(state.shape, state.dtype),
        scratch_shapes=[
            pltpu.VMEM((comps, thetas + 4, axials + 2 * PAD, radial), jnp.float32),
            pltpu.VMEM(state.shape, jnp.float32),
            pltpu.VMEM(flow.shape, jnp.float32),
            pltpu.VMEM((comps, 2 * axials, radial), jnp.float32),
            pltpu.VMEM((2 * axials, 3 * (axials + 2 * PAD)), jnp.bfloat16),
            pltpu.SemaphoreType.DMA((5, thetas)),
        ],
        compiler_params=params(56),
        cost_estimate=cost(40 * state.size, 4 * (3 * state.size + flow.size)),
        name="section",
    )(state, base, flow, before, after, below, above, pole)


def patch(out, lines, rows, place):
    comps, thetas, axials, radial = out.shape
    parts = radial // LANES
    count = rows.shape[0]
    tiles = thetas * axials // 8
    wide = out.reshape(comps, tiles, 8, parts, LANES).transpose(0, 1, 3, 2, 4)
    wide = wide.reshape(comps, tiles, parts, 8, 1, LANES)
    lines = lines.reshape(lines.shape[0], comps, parts, 1, LANES)

    def kernel(rows_ref, place_ref, lines_ref, _, o_ref, sem):
        def copy(n):
            row = rows_ref[n]
            return pltpu.make_async_copy(
                lines_ref.at[place_ref[n]], o_ref.at[:, lax.shift_right_logical(row, 3), :, row & 7], sem
            )

        def start(n, _):
            copy(n).start()
            return 0

        lax.fori_loop(0, count, start, 0, unroll=8)
        pltpu.make_async_copy(
            lines_ref.at[pl.ds(0, count)], lines_ref.at[pl.ds(0, count)], sem
        ).wait()

    wide = pl.pallas_call(
        kernel,
        in_specs=[SMEM, SMEM, ANY, HBM],
        out_specs=HBM,
        out_shape=jax.ShapeDtypeStruct(wide.shape, wide.dtype),
        input_output_aliases={3: 0},
        scratch_shapes=[pltpu.SemaphoreType.DMA],
        compiler_params=params(4),
        cost_estimate=cost(0, 2 * count * comps * radial * 4),
        name="patch",
    )(rows, place, lines, wide)
    wide = wide.reshape(comps, tiles, parts, 8, LANES).transpose(0, 1, 3, 2, 4)
    return wide.reshape(out.shape)

def behind(value, done):
    return lax.optimization_barrier((value, done))

def per_device(state, base, flow, fin, receptor_rows, donor_owner, donor_local, weights):
    comps, thetas, axials, radial = state.shape
    n_az, n_ax = lax.axis_size("az"), lax.axis_size("ax")
    devices = n_az * n_ax
    receptors = receptor_rows.shape[0]
    cap = max(2, 2 * receptors // devices)
    halves = 2 if n_ax % 2 == 0 else 1
    half = n_ax // halves
    spacing = 2.0 * math.pi / (thetas * n_az)
    both = ("az", "ax")
    groups = [
        [a * n_ax + h * half + q for a in range(n_az) for q in range(half)] for h in range(halves)
    ]
    my_half = (lax.axis_index("ax") // half).reshape(1).astype(jnp.int32)

    def exchange(x):
        return lax.all_to_all(x, both, 0, 0, axis_index_groups=groups, tiled=True)

    def around(x, by):
        return lax.ppermute(x, "az", [(a, (a + by) % n_az) for a in range(n_az)])

    def along(x, by):
        return lax.ppermute(x, "ax", [(a, a + by) for a in range(n_ax) if 0 <= a + by < n_ax])

    blocks = [fin]
    if halves == 2:
        blocks.append(lax.ppermute(fin, "ax", [(a, (a + half) % n_ax) for a in range(n_ax)]))
    first, last = theta_edges(state)
    before, after = around(last, 1), around(first, -1)
    owner, first = behind(donor_owner[:, 0], first)
    table, place = requests(
        owner, donor_local, weights, n_az, n_ax, halves, my_half, cap, fin.shape[0]
    )
    asked = exchange(table)
    later, table = behind(state, table)
    low, high, pole = inner_edges(later)
    below, above = along(high, 1), along(low, -1)
    asked, low, before = lax.optimization_barrier((asked, low, before))
    pole = around(pole, n_az // 2)
    lines = interpolate(
        asked[:, 0], [lines_of(b) for b in blocks], halves * cap, comps, radial
    )
    lines, before, after, below, above, pole = lax.optimization_barrier(
        (lines, before, after, below, above, pole)
    )
    base, lines = behind(base, lines)
    lines = exchange(lines)
    out = section(state, base, flow, before, after, below, above, pole, spacing)
    return patch(out, lines, receptor_rows, place.reshape(receptors))

def solution(mesh):
    placed = (
        P(None, "az", "ax", None),
        P(None, "az", "ax", None),
        P("az", "ax", None),
        P(("az", "ax"), None, None),
        P(("az", "ax")),
        P(("az", "ax"), None),
        P(("az", "ax")),
        P(("az", "ax"), None),
    )
    return jax.shard_map(
        per_device, mesh=mesh, in_specs=placed, out_specs=P(None, "az", "ax", None), check_vma=False
    )
```
